256 devices in a mesh: blk: 8 (over x_hi, y), group: 32 (over z, x_lo, core).
Axes of the slice: x: 4 (x_hi: 2, x_lo: 2; x = x_hi * 2 + x_lo), y: 4, z: 8, core: 2. Of those that a mesh axis runs over, the one named last changes fastest.
Arguments:
- walk_rows: bfloat16 [4096, 131072], P('blk', 'group'), may hold values from -6 to 6
- col_values: bfloat16 [49152, 4096], P('group', 'blk'), may hold values from -0.02734375 to 0.02734375
- col_index: int32 [96, 8], P('group'), may hold values from 0 to 7
- col_count: int32 [32, 8], P('group'), may hold values from 1 to 3, as said below
Outputs:
- inflated: float32 [4096, 4096], P(('blk', 'group'))
The draws below stay inside these ranges and needn't reach their ends.
Inputs may be any that keep to these rules, and one draw needn't show every extreme that they name: `col_count`: each list holds 1 to 3 valid slots; some list holds 3; contents of the other slots are arbitrary.
All inputs are finite; a program needn't handle non-finite values.
Results may differ from the reference program's by a relative error of at most 0.0003.
Values may be sent and summed in bfloat16 or wider, within the bound.
No kernel may reach another device: no remote copies, remote signals or barrier semaphores. Data moves between devices by JAX's collectives and lax.ppermute only.
A program may use at most 64 MiB of HBM per device.

```python
import jax
import jax.numpy as jnp
from jax import lax

BS = 512
KG = 8
LMAX = 3
ROWS = 4096
INNER = 131072
COLS = 4096
SLOTS = 96
N_BLK = 8
N_GROUP = 32


def draw_col_count(key, part):
    keys = jax.random.split(key, 3)
    heavy = jax.random.randint(keys[0], (N_GROUP, N_BLK), 0, 4) == 0
    counts = jnp.where(heavy, LMAX, 1)
    row = jax.random.randint(keys[1], (), 0, N_GROUP)
    column = jax.random.randint(keys[2], (), 0, N_BLK)
    counts = counts.at[row, column].set(LMAX)
    return counts.astype(jnp.int32)


def touch_ends(values, stream_key, low, top_value):
    shape = values.shape
    place = [jax.random.randint(jax.random.fold_in(stream_key, axis), (), 0, shape[axis]) for axis in range(len(shape))]
    values = values.at[tuple(place)].set(low)
    longest = shape.index(max(shape))
    place[longest] = (place[longest] + 1) % shape[longest]
    return values.at[tuple(place)].set(top_value)


def spiked(values, own_key, source, target, blocks, factor):
    def block_of(dim):
        return (jnp.arange(values.shape[dim]) // (values.shape[dim] // blocks)).reshape((-1,) + (1,) * (values.ndim - 1 - dim))

    near = jax.random.permutation(own_key, blocks)[block_of(target)]
    far = (block_of(target) + blocks // 2) % blocks
    return jnp.where((block_of(source) == near) | (block_of(source) == far), factor * values, values)


def steps_of(key, dims, shards, smallest, high):
    loudness, own = 1.0, jax.random.fold_in(key, 6)
    for dim, shards_of in shards:
        draws = jnp.exp(jax.random.uniform(jax.random.fold_in(own, dim), (shards_of,), jnp.float32, smallest / len(shards), high / len(shards)))
        loudness = loudness * jnp.repeat(draws, dims[dim] // shards_of).reshape([-1 if axis == dim else 1 for axis in range(len(dims))])
    return loudness


def centred(key, dims, deviation, most, cuts=(), held_as=jnp.bfloat16):
    array = jax.random.normal(key, dims, jnp.float32) * deviation
    if len(cuts) > 0:
        array = steps_of(key, dims, cuts, -0.22, 0.18) * array
    return jnp.clip(array, min=-most, max=most).astype(held_as)


def heavy_noise(stream_key, shape, deviation, most, shards, heavy, kind=jnp.bfloat16):
    drawn = deviation * jax.random.normal(stream_key, shape, jnp.float32)
    if shards:
        drawn = drawn * steps_of(stream_key, shape, shards, -0.22, 0.18)
    return jnp.clip(spiked(drawn, jax.random.fold_in(stream_key, 3), *heavy), -most, most).astype(kind)


def setup_inputs(seed: int = 0) -> dict:
    seeds = jax.random.split(jax.random.key(seed), 5)
    walk_rows = heavy_noise(seeds[0], (ROWS, INNER), 1.0, 6.0, ((0, 8), (1, 32)), (1, 0, 32, 2.75))
    col_values = centred(seeds[1], (SLOTS * BS, COLS), (BS * SLOTS) ** -0.5, 0.02734375, ((0, 32), (1, 8)))
    col_index = touch_ends(jax.random.randint(seeds[2], (SLOTS, N_BLK), 0, KG), jax.random.fold_in(seeds[2], 1), 0, KG - 1).astype(jnp.int32)
    col_count = draw_col_count(jax.random.fold_in(seeds[4], 71), 0)
    return dict(walk_rows=walk_rows, col_values=col_values, col_index=col_index, col_count=col_count)


def reference(walk_rows, col_values, col_index, col_count):
    def panel_product(panel):
        values = lax.dynamic_slice_in_dim(col_values, panel * BS, BS, 1)

        def group_step(total, group):
            for slot in range(LMAX):
                row = (group * LMAX + slot).astype(jnp.int32)
                inner = col_index[row, panel].astype(jnp.int32)
                start = ((group * KG + inner) * BS).astype(jnp.int32)
                block = lax.dynamic_slice_in_dim(walk_rows, start, BS, 1)
                piece = lax.dynamic_slice_in_dim(values, (row * BS).astype(jnp.int32), BS, 0)
                valid = slot < col_count[group, panel]
                product = jnp.dot(block, piece, preferred_element_type=jnp.float32)
                total = total + jnp.where(valid, product, jnp.zeros_like(product))
            return total, None

        total, unused = lax.scan(group_step, jnp.zeros((ROWS, BS), jnp.float32), jnp.arange(N_GROUP, dtype=jnp.int32))
        return total

    parts = lax.map(panel_product, jnp.arange(N_BLK, dtype=jnp.int32))
    expanded = jnp.transpose(parts, (1, 0, 2)).reshape(ROWS, COLS)
    squared = expanded * expanded
    scale = jnp.mean(squared, axis=0) + 1e-6
    return squared / scale
```

```python
import itertools

import jax
import jax.numpy as jnp
import numpy as np
from jax import lax
from jax.experimental import pallas as pl
from jax.experimental.pallas import tpu as pltpu
from jax.sharding import Mesh
from jax.sharding import PartitionSpec as P


AXES = ("xh", "y", "z", "xl", "core")
SIZES = (2, 4, 8, 2, 2)
SLOTS = 3
HALF = 256
F32 = jnp.float32

BATCHES = (
    ((0, 0, 0), (0, 0, 1)),
    ((0, 3, 0), (0, 1, 0), (1, 0, 0)),
    ((0, 3, 1), (0, 1, 1), (1, 0, 1)),
    ((0, 2, 0), (0, 2, 1)),
    ((1, 3, 0), (1, 1, 0), (1, 2, 0)),
    ((1, 3, 1), (1, 1, 1), (1, 2, 1)),
)
ENTRIES = tuple(itertools.chain(*BATCHES))
CORE, ZED, XLO = len(ENTRIES), len(ENTRIES) + 1, len(ENTRIES) + 2


def moves(dxh=0, dy=0, dz=0, dxl=0, dc=0):
    pairs = []
    for at in itertools.product(*(range(n) for n in SIZES)):
        to = [(a + d) % n for a, d, n in zip(at, (dxh, dy, dz, dxl, dc), SIZES)]
        pairs.append((int(np.ravel_multi_index(at, SIZES)), int(np.ravel_multi_index(to, SIZES))))
    return pairs


def send(x, **by):
    return lax.ppermute(x, AXES, moves(**by))


def coordinates():
    dx = np.array([e[0] for e in ENTRIES] + [0] * 3, np.int32)
    dy = np.array([e[1] for e in ENTRIES] + [0] * 3, np.int32)
    spot = np.arange(len(dx), dtype=np.int32)
    xh, y, z, xl, core = (lax.axis_index(name).astype(jnp.int32) for name in AXES)
    meta = ((xh ^ dx) * 4 + ((y + dy) & 3)) * (spot < CORE).astype(np.int32)
    return meta + core * (spot == CORE) + z * (spot == ZED) + xl * (spot == XLO)


def product_body(n, first):
    def body(meta, index, count, w_ref, *refs):
        v_refs, (keep_ref, send_ref, acc_ref) = refs[:n], refs[n:]
        i, s = pl.program_id(0), pl.program_id(1)
        valid = s < count[meta[first + i]]
        for k in range(n):

            @pl.when(jnp.logical_and(i == k, valid))
            def _(k=k):
                part = jnp.dot(w_ref[...], v_refs[k][...], preferred_element_type=F32).reshape(acc_ref.shape)

                @pl.when(s == 0)
                def _():
                    acc_ref[...] = part

                @pl.when(s > 0)
                def _():
                    acc_ref[...] += part

        @pl.when(s == SLOTS - 1)
        def _():
            core = meta[CORE]
            keep_ref[0] = acc_ref[:, core]
            send_ref[0] = acc_ref[:, 1 - core]

    return body


def product(batch, scalars, walk, values):
    n, first = len(BATCHES[batch]), sum(len(b) for b in BATCHES[:batch])
    rows = walk.shape[0]

    def walk_map(i, s, meta, index, count):
        panel = meta[first + i]
        return 0, index[jnp.minimum(s, count[panel] - 1) * 8 + panel]

    def value_map(k, column):
        def at(i, s, meta, index, count):
            last = count[meta[first + k]] - 1
            slot = jnp.where(i == k, jnp.minimum(s, last), jnp.where(i < k, 0, last))
            return slot, column

        return at

    in_specs = [pl.BlockSpec((rows, 512), walk_map)]
    in_specs += [pl.BlockSpec((512, HALF), value_map(k, column)) for k, (_, column) in enumerate(values)]
    out = jax.ShapeDtypeStruct((n, rows // 32, 16, HALF), F32)
    spec = pl.BlockSpec((1, rows // 32, 16, HALF), lambda i, s, *_: (i, 0, 0, 0))
    return pl.pallas_call(
        product_body(n, first),
        out_shape=(out, out),
        grid_spec=pltpu.PrefetchScalarGridSpec(
            num_scalar_prefetch=3,
            grid=(n, SLOTS),
            in_specs=in_specs,
            out_specs=(spec, spec),
            scratch_shapes=[pltpu.VMEM((rows // 32, 2, 16, HALF), F32)],
        ),
        name=f"product{batch}",
    )(*scalars, walk, *(v for v, _ in values))


def core_sum(meta, keep, got):
    n = keep.shape[0]

    def body(meta, keep_ref, got_ref, *outs):
        z = meta[ZED]
        for d in range(8):
            at = pl.ds(2 * ((z + d) & 7), 2)
            outs[d][0] = keep_ref[0, at] + got_ref[0, at]

    spec = pl.BlockSpec((1, 16, 16, HALF), lambda i, *_: (i, 0, 0, 0))
    piece = pl.BlockSpec((1, 2, 16, HALF), lambda i, *_: (i, 0, 0, 0))
    return pl.pallas_call(
        body,
        out_shape=(jax.ShapeDtypeStruct((n, 2, 16, HALF), F32),) * 8,
        grid_spec=pltpu.PrefetchScalarGridSpec(
            num_scalar_prefetch=1, grid=(n,), in_specs=[spec, spec], out_specs=(piece,) * 8
        ),
        name="core_sum",
    )(meta, keep, got)


def z_sum(meta, pieces):
    n = pieces[0].shape[0]

    def body(meta, *refs):
        ins, (keep_ref, send_ref) = refs[:8], refs[8:]
        xl = meta[XLO]
        for ref, at in ((keep_ref, xl), (send_ref, 1 - xl)):
            total = ins[0][:, at]
            for d in range(1, 8):
                total = total + ins[d][:, at]
            ref[...] = total

    out = jax.ShapeDtypeStruct((n, 16, HALF), F32)
    return pl.pallas_call(
        body,
        out_shape=(out, out),
        grid_spec=pltpu.PrefetchScalarGridSpec(
            num_scalar_prefetch=1,
            in_specs=[pl.BlockSpec(memory_space=pltpu.VMEM)] * 8,
            out_specs=(pl.BlockSpec(memory_space=pltpu.VMEM),) * 2,
        ),
        name="z_sum",
    )(meta, *pieces)


def squares(meta, keeps, gots):
    def body(meta, *refs):
        m = len(keeps)
        sq_ref, sum_ref = refs[2 * m :]
        e = 0
        for b in range(m):
            for j in range(keeps[b].shape[0]):
                x = refs[b][j] + refs[m + b][j]
                x = x * x
                at = pl.ds(pl.multiple_of(meta[e] * 512 + ENTRIES[e][2] * HALF, HALF), HALF)
                sq_ref[:, at] = x
                sum_ref[:, at] = jnp.sum(x, axis=0, keepdims=True)
                e += 1

    return pl.pallas_call(
        body,
        out_shape=(jax.ShapeDtypeStruct((16, 4096), F32), jax.ShapeDtypeStruct((1, 4096), F32)),
        grid_spec=pltpu.PrefetchScalarGridSpec(
            num_scalar_prefetch=1,
            in_specs=[pl.BlockSpec(memory_space=pltpu.VMEM)] * (2 * len(keeps)),
            out_specs=(pl.BlockSpec(memory_space=pltpu.VMEM),) * 2,
        ),
        name="squares",
    )(meta, *keeps, *gots)


def on_device(walk, values, col_index, col_count):
    meta = coordinates()
    scalars = (meta, col_index.reshape(-1), col_count.reshape(-1))
    own = (values[:, :HALF], values[:, HALF:])

    up, down, over = [], [], []
    for half in own:
        up.append(send(half, dy=1))
        down.append(send(half, dy=3))
        over.append(send(half, dxh=1))
    far = (send(up[0], dy=1), send(down[1], dy=3))
    over_up = [send(half, dy=1) for half in over]
    over_down = [send(half, dy=3) for half in over]
    over_far = [send(half, dxh=1) for half in far]

    operands = (
        [(values, 0), (values, 1)],
        [(up[0], 0), (down[0], 0), (over[0], 0)],
        [(up[1], 0), (down[1], 0), (over[1], 0)],
        [(far[0], 0), (far[1], 0)],
        [(over_up[0], 0), (over_down[0], 0), (over_far[0], 0)],
        [(over_up[1], 0), (over_down[1], 0), (over_far[1], 0)],
    )
    keeps, gots = [], []
    for batch, given in enumerate(operands):
        keep, give = product(batch, scalars, walk, given)
        pieces = core_sum(meta, keep, send(give, dc=1))
        arrived = [pieces[0]] + [send(pieces[d], dz=d) for d in range(1, 8)]
        keep, give = z_sum(meta, arrived)
        keeps.append(keep)
        gots.append(send(give, dxl=1))

    squared, column = squares(meta, keeps, gots)
    for stage in (
        [dict(dc=1), dict(dxl=1), dict(dc=1, dxl=1)],
        [dict(dz=d) for d in range(1, 8)],
        [dict(dxh=a, dy=b) for a in range(2) for b in range(4) if a + b > 0],
    ):
        column = sum((send(column, **by) for by in stage), column)
    return squared / (column / 4096 + 1e-06)


def solution(mesh):
    fine = Mesh(mesh.devices.reshape(SIZES), AXES)
    blk, group = ("xh", "y"), ("z", "xl", "core")
    return jax.shard_map(
        on_device,
        mesh=fine,
        in_specs=(P(blk, group), P(group, blk), P(group, None), P(group, None)),
        out_specs=P((*blk, *group), None),
        check_vma=False,
    )
```

```python
import itertools

import jax
import jax.numpy as jnp
import numpy as np
from jax import lax
from jax.experimental import pallas as pl
from jax.experimental.pallas import tpu as pltpu
from jax.sharding import Mesh
from jax.sharding import PartitionSpec as P


AXES = ("xh", "y", "z", "xl", "core")
SIZES = (2, 4, 8, 2, 2)
SLOTS = 3
WIDTH = 512
HALF = 256
F32 = jnp.float32
WIRE = jnp.float16
GAIN = 128.0

BATCHES = (
    ((0, 0, (0, 1)),),
    ((0, 3, (0, 1)), (0, 1, (0, 1)), (1, 0, (0, 1))),
    ((0, 2, (0, 1)),),
    ((1, 3, (0,)), (1, 1, (0,)), (1, 2, (0,))),
    ((1, 3, (1,)), (1, 1, (1,)), (1, 2, (1,))),
)
PANELS = tuple(itertools.chain(*BATCHES))
CORE = len(PANELS)


def moves(dxh=0, dy=0, dz=0, dxl=0, dc=0):
    pairs = []
    for at in itertools.product(*(range(n) for n in SIZES)):
        to = [(a + d) % n for a, d, n in zip(at, (dxh, dy, dz, dxl, dc), SIZES)]
        pairs.append((int(np.ravel_multi_index(at, SIZES)), int(np.ravel_multi_index(to, SIZES))))
    return pairs


def send(x, **by):
    return lax.ppermute(x, AXES, moves(**by))


def coordinates():
    dx = np.array([p[0] for p in PANELS] + [0], np.int32)
    dy = np.array([p[1] for p in PANELS] + [0], np.int32)
    is_core = (np.arange(len(dx)) == CORE).astype(np.int32)
    xh, y, core = (lax.axis_index(name).astype(jnp.int32) for name in ("xh", "y", "core"))
    return ((xh ^ dx) * 4 + ((y + dy) & 3)) * (1 - is_core) + core * is_core


def product(batch, scalars, walk, values):
    panels = BATCHES[batch]
    first = sum(len(b) for b in BATCHES[:batch])
    rows = walk.shape[0]
    arrays = []
    pieces = []
    for given in values:
        for array, column, width in given:
            known = [i for i, a in enumerate(arrays) if a is array]
            if not known:
                arrays.append(array)
            pieces.append((known[0] if known else len(arrays) - 1, column, width))
    per_panel = [len(given) for given in values]
    starts = np.cumsum([0] + per_panel)
    halves = sum(p[2] for p in pieces) // HALF
    widest = max(p[2] for p in pieces)
    n = len(panels)

    def body(meta, index, count, w_hbm, *refs):
        v_hbm = refs[: len(arrays)]
        keep_ref, send_ref, w_buf, v_buf, acc_ref, w_sem, v_sem = refs[len(arrays) :]

        def w_copy(k, s):
            block = index[s * 8 + meta[first + k]]
            source = w_hbm.at[:, pl.ds(pl.multiple_of(block * WIDTH, WIDTH), WIDTH)]
            return pltpu.make_async_copy(source, w_buf.at[k * SLOTS + s], w_sem.at[k * SLOTS + s])

        def v_copy(p, s):
            array, column, width = pieces[p]
            source = v_hbm[array].at[pl.ds(s * WIDTH, WIDTH), pl.ds(column, width)]
            return pltpu.make_async_copy(source, v_buf.at[p * SLOTS + s, :, pl.ds(0, width)], v_sem.at[p * SLOTS + s])

        def each(k, s, act):
            if s == 0:
                act()
            else:
                pl.when(s < count[meta[first + k]])(act)

        for k in range(n):
            for s in range(SLOTS):

                def begin(k=k, s=s):
                    w_copy(k, s).start()
                    for p in range(starts[k], starts[k + 1]):
                        v_copy(p, s).start()

                each(k, s, begin)

        core = meta[CORE]
        half = 0
        for k in range(n):
            for p in range(starts[k], starts[k + 1]):
                width = pieces[p][2]
                for s in range(SLOTS):

                    def add(k=k, s=s, p=p, width=width):
                        if p == starts[k]:
                            w_copy(k, s).wait()
                        v_copy(p, s).wait()
                        part = jnp.dot(
                            w_buf[k * SLOTS + s], v_buf[p * SLOTS + s, :, :width], preferred_element_type=F32
                        ).reshape(rows // 64, 2, 2, 16, width)
                        if s == 0:
                            acc_ref[..., :width] = part
                        else:
                            acc_ref[..., :width] += part

                    each(k, s, add)
                for column in range(0, width, HALF):
                    keep_ref[:, half] = acc_ref[:, :, core, :, column : column + HALF]
                    send_ref[:, half] = acc_ref[:, :, 1 - core, :, column : column + HALF]
                    half += 1

    out = jax.ShapeDtypeStruct((rows // 64, halves, 2, 16, HALF), F32)
    blank = pl.BlockSpec(memory_space=pl.ANY)
    whole = pl.BlockSpec(memory_space=pltpu.VMEM)
    return pl.pallas_call(
        body,
        out_shape=(out, out),
        grid_spec=pltpu.PrefetchScalarGridSpec(
            num_scalar_prefetch=3,
            in_specs=[blank] * (1 + len(arrays)),
            out_specs=(whole, whole),
            scratch_shapes=[
                pltpu.VMEM((n * SLOTS, rows, WIDTH), walk.dtype),
                pltpu.VMEM((len(pieces) * SLOTS, WIDTH, widest), walk.dtype),
                pltpu.VMEM((rows // 64, 2, 2, 16, widest), F32),
                pltpu.SemaphoreType.DMA((n * SLOTS,)),
                pltpu.SemaphoreType.DMA((len(pieces) * SLOTS,)),
            ],
        ),
        name=f"product{batch}",
    )(*scalars, walk, *arrays)


def squares(meta, keeps, gots):
    spots = [(p, half) for p, panel in enumerate(PANELS) for half in panel[2]]

    def body(meta, *refs):
        m = len(keeps)
        sq_ref, sum_ref, row_ref = refs[2 * m :]
        e = 0
        for b in range(m):
            for j in range(keeps[b].shape[0]):
                x = refs[b][j] + refs[m + b][j]
                x = x * x
                p, half = spots[e]
                at = pl.multiple_of(meta[p] * WIDTH + half * HALF, HALF)
                sq_ref[:, pl.ds(at, HALF)] = x
                total = jnp.sum(x, axis=0, keepdims=True)
                row_ref[pl.ds(at // 128, 1)] = total[:, :128]
                row_ref[pl.ds(at // 128 + 1, 1)] = total[:, 128:]
                e += 1
        sum_ref[...] = jnp.broadcast_to(row_ref[...][None], sum_ref.shape)

    whole = pl.BlockSpec(memory_space=pltpu.VMEM)
    return pl.pallas_call(
        body,
        out_shape=(jax.ShapeDtypeStruct((16, 4096), F32), jax.ShapeDtypeStruct((16, 32, 128), F32)),
        grid_spec=pltpu.PrefetchScalarGridSpec(
            num_scalar_prefetch=1,
            in_specs=[whole] * (2 * len(keeps)),
            out_specs=(whole, whole),
            scratch_shapes=[pltpu.VMEM((32, 128), F32)],
        ),
        name="squares",
    )(meta, *keeps, *gots)


def scaled(squared, sums):
    def body(sq_ref, sum_ref, out_ref):
        total = sum_ref[0]
        for t in range(1, sums.shape[0]):
            total = total + sum_ref[t]
        scale = total / 4096 + 1e-06
        for r in range(32):
            at = slice(r * 128, r * 128 + 128)
            out_ref[:, at] = sq_ref[:, at] / scale[r : r + 1]

    return pl.pallas_call(body, out_shape=jax.ShapeDtypeStruct(squared.shape, F32), name="scaled")(squared, sums)


def on_device(walk, values, col_index, col_count):
    meta = coordinates()
    scalars = (meta, col_index.reshape(-1), col_count.reshape(-1))
    xl = lax.axis_index("xl")

    def whole(array):
        return [(array, 0, WIDTH)]

    def pair(left, right):
        return [(left, 0, HALF), (right, 0, HALF)]

    def one(array):
        return [(array, 0, HALF)]

    def z_stage(keep, got, scalars):
        pieces = ((keep + got) * GAIN).astype(WIRE)
        pieces, *scalars = lax.optimization_barrier((pieces, *scalars))
        return scalars, lax.all_to_all(pieces, "z", 0, 0)

    def xl_stage(arrived):
        total = jnp.sum(arrived.astype(F32), axis=0) * (1 / GAIN)
        keep = lax.dynamic_index_in_dim(total, xl, 1, keepdims=False)
        give = lax.dynamic_index_in_dim(total, 1 - xl, 1, keepdims=False)
        return keep, send(give, dxl=1)

    up = send(values, dy=1)
    down = send(values, dy=3)
    over = send(values, dxh=1)

    ends = []

    def work(batch, given, scalars):
        keep, give = product(batch, scalars, walk, given)
        scalars, arrived = z_stage(keep, send(give, dc=1), scalars)
        ends.append(xl_stage(arrived))
        return scalars

    last = work(0, [whole(values)], scalars)
    far = (send(up[:, :HALF], dy=1), send(down[:, HALF:], dy=3))
    over_half = (over[:, :HALF], over[:, HALF:])
    over_up = [send(half, dy=1) for half in over_half]
    over_down = [send(half, dy=3) for half in over_half]
    last = work(1, [whole(up), whole(down), whole(over)], last)
    over_far = [send(half, dxh=1) for half in far]
    last = work(2, [pair(*far)], last)
    for t in range(2):
        last = work(3 + t, [one(over_up[t]), one(over_down[t]), one(over_far[t])], last)

    squared, sums = squares(meta, [e[0] for e in ends], [e[1] for e in ends])
    sums = jnp.sum(lax.all_to_all(sums, ("z", "core"), 0, 0), axis=0)
    sums = lax.all_to_all(jnp.broadcast_to(sums[None], (16, 32, 128)), ("xh", "y", "xl"), 0, 0)
    return scaled(squared, sums)


def solution(mesh):
    fine = Mesh(mesh.devices.reshape(SIZES), AXES)
    blk, group = ("xh", "y"), ("z", "xl", "core")
    return jax.shard_map(
        on_device,
        mesh=fine,
        in_specs=(P(blk, group), P(group, blk), P(group, None), P(group, None)),
        out_specs=P((*blk, *group), None),
        check_vma=False,
    )
```

```python
import itertools

import jax
import jax.numpy as jnp
import numpy as np
from jax import lax
from jax.experimental import pallas as pl
from jax.experimental.pallas import tpu as pltpu
from jax.sharding import Mesh
from jax.sharding import PartitionSpec as P


AXES = ("xh", "y", "z", "xl", "core")
SIZES = (2, 4, 8, 2, 2)
SLOTS = 3
WIDTH = 512
HALF = 256
F32 = jnp.float32
WIRE = jnp.float16
TOP = 60000.0
SCALE = 64.0

BATCHES = (
    ((0, 0, (0, 1)),),
    ((0, 3, (0, 1)), (0, 1, (0, 1)), (1, 0, (0, 1))),
    ((0, 2, (0, 1)), (1, 3, (0,)), (1, 1, (0,)), (1, 2, (0,))),
    ((1, 3, (1,)), (1, 1, (1,)), (1, 2, (1,))),
)
PANELS = tuple(itertools.chain(*BATCHES))
CORE = len(PANELS)


def moves(dxh=0, dy=0, dz=0, dxl=0, dc=0):
    pairs = []
    for at in itertools.product(*(range(n) for n in SIZES)):
        to = [(a + d) % n for a, d, n in zip(at, (dxh, dy, dz, dxl, dc), SIZES)]
        pairs.append((int(np.ravel_multi_index(at, SIZES)), int(np.ravel_multi_index(to, SIZES))))
    return pairs


def send(x, **by):
    return lax.ppermute(x, AXES, moves(**by))


def coordinates():
    dx = np.array([p[0] for p in PANELS] + [0], np.int32)
    dy = np.array([p[1] for p in PANELS] + [0], np.int32)
    is_core = (np.arange(len(dx)) == CORE).astype(np.int32)
    xh, y, core = (lax.axis_index(name).astype(jnp.int32) for name in ("xh", "y", "core"))
    return ((xh ^ dx) * 4 + ((y + dy) & 3)) * (1 - is_core) + core * is_core


def product(batch, scalars, walk, values):
    panels = BATCHES[batch]
    first = sum(len(b) for b in BATCHES[:batch])
    rows = walk.shape[0]
    arrays = []
    pieces = []
    for given in values:
        for array, column, width in given:
            known = [i for i, a in enumerate(arrays) if a is array]
            if not known:
                arrays.append(array)
            pieces.append((known[0] if known else len(arrays) - 1, column, width))
    per_panel = [len(given) for given in values]
    starts = np.cumsum([0] + per_panel)
    halves = sum(p[2] for p in pieces) // HALF
    widest = max(p[2] for p in pieces)
    n = len(panels)

    def body(meta, index, count, w_hbm, *refs):
        v_hbm = refs[: len(arrays)]
        keep_ref, send_ref, w_buf, v_buf, acc_ref, w_sem, v_sem = refs[len(arrays) :]

        def w_copy(k, s):
            block = index[s * 8 + meta[first + k]]
            source = w_hbm.at[:, pl.ds(pl.multiple_of(block * WIDTH, WIDTH), WIDTH)]
            return pltpu.make_async_copy(source, w_buf.at[k * SLOTS + s], w_sem.at[k * SLOTS + s])

        def v_copy(p, s):
            array, column, width = pieces[p]
            source = v_hbm[array].at[pl.ds(s * WIDTH, WIDTH), pl.ds(column, width)]
            return pltpu.make_async_copy(source, v_buf.at[p * SLOTS + s, :, pl.ds(0, width)], v_sem.at[p * SLOTS + s])

        def each(k, s, act):
            if s == 0:
                act()
            else:
                pl.when(s < count[meta[first + k]])(act)

        for k in range(n):
            for s in range(SLOTS):

                def begin(k=k, s=s):
                    w_copy(k, s).start()
                    for p in range(starts[k], starts[k + 1]):
                        v_copy(p, s).start()

                each(k, s, begin)

        core = meta[CORE]
        half = 0
        for k in range(n):
            for p in range(starts[k], starts[k + 1]):
                width = pieces[p][2]
                for s in range(SLOTS):

                    def add(k=k, s=s, p=p, width=width):
                        if p == starts[k]:
                            w_copy(k, s).wait()
                        v_copy(p, s).wait()
                        part = jnp.dot(
                            w_buf[k * SLOTS + s], v_buf[p * SLOTS + s, :, :width], preferred_element_type=F32
                        ).reshape(rows // 64, 2, 2, 16, width)
                        if s == 0:
                            acc_ref[..., :width] = part
                        else:
                            acc_ref[..., :width] += part

                    each(k, s, add)
                for column in range(0, width, HALF):
                    keep_ref[:, half] = acc_ref[:, :, core, :, column : column + HALF]
                    send_ref[:, half] = acc_ref[:, :, 1 - core, :, column : column + HALF]
                    half += 1

    out = jax.ShapeDtypeStruct((rows // 64, halves, 2, 16, HALF), F32)
    blank = pl.BlockSpec(memory_space=pl.ANY)
    whole = pl.BlockSpec(memory_space=pltpu.VMEM)
    return pl.pallas_call(
        body,
        out_shape=(out, out),
        grid_spec=pltpu.PrefetchScalarGridSpec(
            num_scalar_prefetch=3,
            in_specs=[blank] * (1 + len(arrays)),
            out_specs=(whole, whole),
            scratch_shapes=[
                pltpu.VMEM((n * SLOTS, rows, WIDTH), walk.dtype),
                pltpu.VMEM((len(pieces) * SLOTS, WIDTH, widest), walk.dtype),
                pltpu.VMEM((rows // 64, 2, 2, 16, widest), F32),
                pltpu.SemaphoreType.DMA((n * SLOTS,)),
                pltpu.SemaphoreType.DMA((len(pieces) * SLOTS,)),
            ],
        ),
    )(*scalars, walk, *arrays)


def squares(meta, keeps, gots):
    spots = [(p, half) for p, panel in enumerate(PANELS) for half in panel[2]]

    def body(meta, *refs):
        m = len(keeps)
        sq_ref, sum_ref, row_ref = refs[2 * m :]
        e = 0
        for b in range(m):
            for j in range(keeps[b].shape[0]):
                x = refs[b][j] + refs[m + b][j]
                x = x * x
                p, half = spots[e]
                at = pl.multiple_of(meta[p] * WIDTH + half * HALF, HALF)
                sq_ref[:, pl.ds(at, HALF)] = x
                total = jnp.sum(x, axis=0, keepdims=True)
                row_ref[pl.ds(at // 128, 1)] = total[:, :128]
                row_ref[pl.ds(at // 128 + 1, 1)] = total[:, 128:]
                e += 1
        sum_ref[...] = jnp.broadcast_to(row_ref[...][None], sum_ref.shape)

    whole = pl.BlockSpec(memory_space=pltpu.VMEM)
    return pl.pallas_call(
        body,
        out_shape=(jax.ShapeDtypeStruct((16, 4096), F32), jax.ShapeDtypeStruct((16, 32, 128), F32)),
        grid_spec=pltpu.PrefetchScalarGridSpec(
            num_scalar_prefetch=1,
            in_specs=[whole] * (2 * len(keeps)),
            out_specs=(whole, whole),
            scratch_shapes=[pltpu.VMEM((32, 128), F32)],
        ),
        name="squares",
    )(meta, *keeps, *gots)


def scaled(squared, sums):
    def body(sq_ref, sum_ref, out_ref):
        total = sum_ref[0]
        for t in range(1, sums.shape[0]):
            total = total + sum_ref[t]
        scale = total / 4096 + 1e-06
        for r in range(32):
            at = slice(r * 128, r * 128 + 128)
            out_ref[:, at] = sq_ref[:, at] / scale[r : r + 1]

    return pl.pallas_call(body, out_shape=jax.ShapeDtypeStruct(squared.shape, F32), name="scaled")(squared, sums)


def encode(total):
    n = total.shape[1]
    top = jnp.max(jnp.abs(total), axis=(0, 2, 3))
    scale = lax.reduce_precision(jnp.maximum(top * (SCALE * 1.002), 6.2e-05), 5, 10)
    t = total * (SCALE / scale)[None, :, None, None]
    codes = (t * jnp.abs(t) * TOP).astype(WIRE).reshape(8, n * 32, HALF)
    rows = jnp.pad(scale.astype(WIRE), ((0, 16 - n), (0, 0)))
    return jnp.concatenate([codes, jnp.broadcast_to(rows[None], (8, 16, HALF))], axis=1)


def decode(coded, n):
    codes = coded[:, : n * 32].astype(F32).reshape(8, n, 2, 16, HALF)
    scale = coded[:, n * 32 : n * 33].astype(F32) * (1 / SCALE)
    size = jnp.sqrt(jnp.abs(codes) * (1 / TOP))
    return jnp.sum(jnp.where(codes < 0, -size, size) * scale[:, :, None, None], axis=0)


def pipeline(walk, values, col_index, col_count):
    meta = coordinates()
    scalars = (meta, col_index.reshape(-1), col_count.reshape(-1))
    xl = lax.axis_index("xl")

    def move(x, **by):
        return send(x, **by)

    def whole(array):
        return [(array, 0, WIDTH)]

    def pair(left, right):
        return [(left, 0, HALF), (right, 0, HALF)]

    def one(array):
        return [(array, 0, HALF)]

    ends = []

    def work(batch, given):
        keep, give = product(batch, scalars, walk, given)
        got = move(give, dc=1)
        arrived = lax.all_to_all(encode(keep + got), "z", 0, 0, tiled=True)
        total = decode(arrived, keep.shape[1])
        mine = lax.dynamic_index_in_dim(total, xl, 1, keepdims=False)
        other = lax.dynamic_index_in_dim(total, 1 - xl, 1, keepdims=False)
        ends.append((mine, move(other, dxl=1)))

    up = move(values, dy=1)
    down = move(values, dy=3)
    over = move(values, dxh=1)
    far = [move(up[:, :HALF], dy=1), move(down[:, HALF:], dy=3)]
    over_half = (over[:, :HALF], over[:, HALF:])
    over_up = [move(over_half[t], dy=1) for t in range(2)]
    over_down = [move(over_half[t], dy=3) for t in range(2)]
    over_far = [move(far[t], dxh=1) for t in range(2)]

    work(0, [whole(values)])
    work(1, [whole(up), whole(down), whole(over)])
    work(2, [pair(*far), one(over_up[0]), one(over_down[0]), one(over_far[0])])
    work(3, [one(over_up[1]), one(over_down[1]), one(over_far[1])])

    squared, sums = squares(meta, [e[0] for e in ends], [e[1] for e in ends])
    sums = jnp.sum(lax.all_to_all(sums, ("z", "core"), 0, 0), axis=0)
    sums = lax.all_to_all(jnp.broadcast_to(sums[None], (16, 32, 128)), ("xh", "y", "xl"), 0, 0)
    return scaled(squared, sums)


def solution(mesh):
    fine = Mesh(mesh.devices.reshape(SIZES), AXES)
    blk, group = ("xh", "y"), ("z", "xl", "core")
    return jax.shard_map(
        pipeline,
        mesh=fine,
        in_specs=(P(blk, group), P(group, blk), P(group, None), P(group, None)),
        out_specs=P((*blk, *group), None),
        check_vma=False,
    )
```

```python
import itertools

import jax
import jax.numpy as jnp
import numpy as np
from jax import lax
from jax.experimental import pallas as pl
from jax.experimental.pallas import tpu as pltpu
from jax.sharding import Mesh
from jax.sharding import PartitionSpec as P


AXES = ("xh", "y", "z", "xl", "core")
SIZES = (2, 4, 8, 2, 2)
SLOTS = 3
WIDTH = 512
HALF = 256
F32 = jnp.float32
WIRE = jnp.float16
TOP = 60000.0
SCALE = 64.0

BATCHES = (
    ((0, 0, (0, 1)),),
    ((0, 3, (0, 1)), (0, 1, (0, 1)), (1, 0, (0, 1))),
    ((0, 2, (0, 1)), (1, 3, (0,)), (1, 1, (0,)), (1, 2, (0,))),
    ((1, 3, (1,)), (1, 1, (1,)), (1, 2, (1,))),
)
PANELS = tuple(itertools.chain(*BATCHES))
CORE, XLO = len(PANELS), len(PANELS) + 1


def moves(dxh=0, dy=0, dz=0, dxl=0, dc=0):
    pairs = []
    for at in itertools.product(*(range(n) for n in SIZES)):
        to = [(a + d) % n for a, d, n in zip(at, (dxh, dy, dz, dxl, dc), SIZES)]
        pairs.append((int(np.ravel_multi_index(at, SIZES)), int(np.ravel_multi_index(to, SIZES))))
    return pairs


def send(x, **by):
    return lax.ppermute(x, AXES, moves(**by))


def coordinates():
    dx = np.array([p[0] for p in PANELS] + [0, 0], np.int32)
    dy = np.array([p[1] for p in PANELS] + [0, 0], np.int32)
    spot = np.arange(len(dx), dtype=np.int32)
    xh, y, xl, core = (lax.axis_index(name).astype(jnp.int32) for name in ("xh", "y", "xl", "core"))
    panels = ((xh ^ dx) * 4 + ((y + dy) & 3)) * (spot < CORE).astype(np.int32)
    return panels + core * (spot == CORE) + xl * (spot == XLO)


def product(batch, scalars, walk, values, xl_first):
    panels = BATCHES[batch]
    first = sum(len(b) for b in BATCHES[:batch])
    rows = walk.shape[0]
    arrays = []
    pieces = []
    for given in values:
        for array, column, width in given:
            known = [i for i, a in enumerate(arrays) if a is array]
            if not known:
                arrays.append(array)
            pieces.append((known[0] if known else len(arrays) - 1, column, width))
    per_panel = [len(given) for given in values]
    starts = np.cumsum([0] + per_panel)
    halves = sum(p[2] for p in pieces) // HALF
    widest = max(p[2] for p in pieces)
    n = len(panels)

    def body(meta, index, count, w_hbm, *refs):
        v_hbm = refs[: len(arrays)]
        keep_ref, send_ref, w_buf, v_buf, acc_ref, w_sem, v_sem = refs[len(arrays) :]

        def w_copy(k, s):
            block = index[s * 8 + meta[first + k]]
            source = w_hbm.at[:, pl.ds(pl.multiple_of(block * WIDTH, WIDTH), WIDTH)]
            return pltpu.make_async_copy(source, w_buf.at[k * SLOTS + s], w_sem.at[k * SLOTS + s])

        def v_copy(p, s):
            array, column, width = pieces[p]
            source = v_hbm[array].at[pl.ds(s * WIDTH, WIDTH), pl.ds(column, width)]
            return pltpu.make_async_copy(source, v_buf.at[p * SLOTS + s, :, pl.ds(0, width)], v_sem.at[p * SLOTS + s])

        def each(k, s, act):
            if s == 0:
                act()
            else:
                pl.when(s < count[meta[first + k]])(act)

        for k in range(n):
            for s in range(SLOTS):

                def begin(k=k, s=s):
                    w_copy(k, s).start()
                    for p in range(starts[k], starts[k + 1]):
                        v_copy(p, s).start()

                each(k, s, begin)

        core, xl = meta[CORE], meta[XLO]
        half = 0
        for k in range(n):
            for p in range(starts[k], starts[k + 1]):
                width = pieces[p][2]
                for s in range(SLOTS):

                    def add(k=k, s=s, p=p, width=width):
                        if p == starts[k]:
                            w_copy(k, s).wait()
                        v_copy(p, s).wait()
                        part = jnp.dot(
                            w_buf[k * SLOTS + s], v_buf[p * SLOTS + s, :, :width], preferred_element_type=F32
                        ).reshape(rows // 64, 2, 2, 16, width)
                        if s == 0:
                            acc_ref[..., :width] = part
                        else:
                            acc_ref[..., :width] += part

                    each(k, s, add)
                for column in range(0, width, HALF):
                    for r, at in ((0, xl), (1, 1 - xl)):
                        to = (r, slice(None), half) if xl_first else (slice(None), r, half)
                        keep_ref[to] = acc_ref[:, at, core, :, column : column + HALF]
                        send_ref[to] = acc_ref[:, at, 1 - core, :, column : column + HALF]
                    half += 1

    lead = (2, rows // 64) if xl_first else (rows // 64, 2)
    out = jax.ShapeDtypeStruct((*lead, halves, 16, HALF), F32)
    blank = pl.BlockSpec(memory_space=pl.ANY)
    whole = pl.BlockSpec(memory_space=pltpu.VMEM)
    return pl.pallas_call(
        body,
        out_shape=(out, out),
        grid_spec=pltpu.PrefetchScalarGridSpec(
            num_scalar_prefetch=3,
            in_specs=[blank] * (1 + len(arrays)),
            out_specs=(whole, whole),
            scratch_shapes=[
                pltpu.VMEM((n * SLOTS, rows, WIDTH), walk.dtype),
                pltpu.VMEM((len(pieces) * SLOTS, WIDTH, widest), walk.dtype),
                pltpu.VMEM((rows // 64, 2, 2, 16, widest), F32),
                pltpu.SemaphoreType.DMA((n * SLOTS,)),
                pltpu.SemaphoreType.DMA((len(pieces) * SLOTS,)),
            ],
        ),
    )(*scalars, walk, *arrays)


def squares(meta, ends):
    spots = [(p, half) for p, panel in enumerate(PANELS) for half in panel[2]]
    terms = [len(end) for end in ends]

    def body(meta, *refs):
        sq_ref, sum_ref, row_ref = refs[sum(terms) :]
        e = first = 0
        for m in terms:
            for j in range(refs[first].shape[0]):
                x = refs[first][j]
                for k in range(1, m):
                    x = x + refs[first + k][j]
                x = x * x
                p, half = spots[e]
                at = pl.multiple_of(meta[p] * WIDTH + half * HALF, HALF)
                sq_ref[:, pl.ds(at, HALF)] = x
                total = jnp.sum(x, axis=0, keepdims=True)
                row_ref[pl.ds(at // 128, 1)] = total[:, :128]
                row_ref[pl.ds(at // 128 + 1, 1)] = total[:, 128:]
                e += 1
            first += m
        sum_ref[...] = jnp.broadcast_to(row_ref[...][None], sum_ref.shape)

    whole = pl.BlockSpec(memory_space=pltpu.VMEM)
    return pl.pallas_call(
        body,
        out_shape=(jax.ShapeDtypeStruct((16, 4096), F32), jax.ShapeDtypeStruct((16, 32, 128), F32)),
        grid_spec=pltpu.PrefetchScalarGridSpec(
            num_scalar_prefetch=1,
            in_specs=[whole] * sum(terms),
            out_specs=(whole, whole),
            scratch_shapes=[pltpu.VMEM((32, 128), F32)],
        ),
        name="squares",
    )(meta, *itertools.chain(*ends))


def scaled(squared, sums):
    def body(sq_ref, sum_ref, out_ref):
        total = sum_ref[0]
        for t in range(1, sums.shape[0]):
            total = total + sum_ref[t]
        scale = total / 4096 + 1e-06
        for r in range(32):
            at = slice(r * 128, r * 128 + 128)
            out_ref[:, at] = sq_ref[:, at] / scale[r : r + 1]

    return pl.pallas_call(body, out_shape=jax.ShapeDtypeStruct(squared.shape, F32), name="scaled")(squared, sums)


def encode(total):
    n = total.shape[-3]
    top = jnp.max(jnp.abs(total), axis=(*range(total.ndim - 3), total.ndim - 2))
    scale = lax.reduce_precision(jnp.maximum(top * (SCALE * 1.002), 6.2e-05), 5, 10)
    t = total * (SCALE / scale)[:, None]
    codes = (t * jnp.abs(t) * TOP).astype(WIRE).reshape(8, -1, HALF)
    rows = jnp.pad(scale.astype(WIRE), ((0, 16 - n), (0, 0)))
    return jnp.concatenate([codes, jnp.broadcast_to(rows[None], (8, 16, HALF))], axis=1)


def decode(coded, shape):
    end = coded.shape[1] - 16
    codes = coded[:, :end].astype(F32).reshape(8, *shape)
    scale = coded[:, end : end + shape[-3]].astype(F32) * (1 / SCALE)
    scale = scale.reshape(8, *([1] * (len(shape) - 3)), shape[-3], 1, HALF)
    size = jnp.sqrt(jnp.abs(codes) * (1 / TOP))
    return jnp.sum(jnp.where(codes < 0, -size, size) * scale, axis=0)


def pipeline(walk, values, col_index, col_count):
    meta = coordinates()
    scalars = (meta, col_index.reshape(-1), col_count.reshape(-1))

    def move(x, **by):
        return send(x, **by)

    def whole(array):
        return [(array, 0, WIDTH)]

    def pair(left, right):
        return [(left, 0, HALF), (right, 0, HALF)]

    def one(array):
        return [(array, 0, HALF)]

    ends = []

    def work(batch, given, xl_first=False):
        keep, give = product(batch, scalars, walk, given, xl_first)
        got = move(give, dc=1)
        n = keep.shape[2]
        if xl_first:
            other = move(keep[1] + got[1], dxl=1)
            arrived = lax.all_to_all(encode(keep[0] + got[0] + other), "z", 0, 0, tiled=True)
            ends.append((decode(arrived, (n, 16, HALF)),))
        else:
            arrived = lax.all_to_all(encode(keep + got), "z", 0, 0, tiled=True)
            total = decode(arrived, (2, n, 16, HALF))
            ends.append((total[0], move(total[1], dxl=1)))

    up = move(values, dy=1)
    down = move(values, dy=3)
    over = move(values, dxh=1)
    far = [move(up[:, :HALF], dy=1), move(down[:, HALF:], dy=3)]
    over_half = (over[:, :HALF], over[:, HALF:])
    over_up = [move(over_half[t], dy=1) for t in range(2)]
    over_down = [move(over_half[t], dy=3) for t in range(2)]
    over_far = [move(far[t], dxh=1) for t in range(2)]

    work(0, [whole(values)])
    work(1, [whole(up), whole(down), whole(over)])
    work(2, [pair(*far), one(over_up[0]), one(over_down[0]), one(over_far[0])])
    work(3, [one(over_up[1]), one(over_down[1]), one(over_far[1])], xl_first=True)

    squared, sums = squares(meta, ends)
    sums = jnp.sum(lax.all_to_all(sums, ("z", "core"), 0, 0), axis=0)
    sums = lax.all_to_all(jnp.broadcast_to(sums[None], (16, 32, 128)), ("xh", "y", "xl"), 0, 0)
    return scaled(squared, sums)


def solution(mesh):
    fine = Mesh(mesh.devices.reshape(SIZES), AXES)
    blk, group = ("xh", "y"), ("z", "xl", "core")
    return jax.shard_map(
        pipeline,
        mesh=fine,
        in_specs=(P(blk, group), P(group, blk), P(group, None), P(group, None)),
        out_specs=P((*blk, *group), None),
        check_vma=False,
    )
```

```python
import itertools

import jax
import jax.numpy as jnp
import numpy as np
from jax import lax
from jax.experimental import pallas as pl
from jax.experimental.pallas import tpu as pltpu
from jax.sharding import Mesh
from jax.sharding import PartitionSpec as P


AXES = ("xh", "y", "z", "xl", "core")
SIZES = (2, 4, 8, 2, 2)
SLOTS = 3
WIDTH = 512
HALF = 256
F32 = jnp.float32
WIRE = jnp.float16
TOP = 60000.0
SCALE = 64.0

BATCHES = (
    ((0, 0, (0, 1)),),
    ((0, 3, (0, 1)), (0, 1, (0, 1)), (1, 0, (0, 1))),
    ((0, 2, (0, 1)), (1, 3, (0,)), (1, 1, (0,)), (1, 2, (0,))),
    ((1, 3, (1,)), (1, 1, (1,)), (1, 2, (1,))),
)
PANELS = tuple(itertools.chain(*BATCHES))
CORE = len(PANELS)


def moves(dxh=0, dy=0, dz=0, dxl=0, dc=0):
    pairs = []
    for at in itertools.product(*(range(n) for n in SIZES)):
        to = [(a + d) % n for a, d, n in zip(at, (dxh, dy, dz, dxl, dc), SIZES)]
        pairs.append((int(np.ravel_multi_index(at, SIZES)), int(np.ravel_multi_index(to, SIZES))))
    return pairs


def send(x, **by):
    return lax.ppermute(x, AXES, moves(**by))


def coordinates():
    dx = np.array([p[0] for p in PANELS] + [0], np.int32)
    dy = np.array([p[1] for p in PANELS] + [0], np.int32)
    is_core = (np.arange(len(dx)) == CORE).astype(np.int32)
    xh, y, core = (lax.axis_index(name).astype(jnp.int32) for name in ("xh", "y", "core"))
    return ((xh ^ dx) * 4 + ((y + dy) & 3)) * (1 - is_core) + core * is_core


def product(batch, scalars, walk, values):
    panels = BATCHES[batch]
    first = sum(len(b) for b in BATCHES[:batch])
    rows = walk.shape[0]
    arrays = []
    pieces = []
    for given in values:
        for array, column, width in given:
            known = [i for i, a in enumerate(arrays) if a is array]
            if not known:
                arrays.append(array)
            pieces.append((known[0] if known else len(arrays) - 1, column, width))
    per_panel = [len(given) for given in values]
    starts = np.cumsum([0] + per_panel)
    halves = sum(p[2] for p in pieces) // HALF
    widest = max(p[2] for p in pieces)
    n = len(panels)

    def body(meta, index, count, w_hbm, *refs):
        v_hbm = refs[: len(arrays)]
        keep_ref, send_ref, w_buf, v_buf, acc_ref, w_sem, v_sem = refs[len(arrays) :]

        def w_copy(k, s):
            block = index[s * 8 + meta[first + k]]
            source = w_hbm.at[:, pl.ds(pl.multiple_of(block * WIDTH, WIDTH), WIDTH)]
            return pltpu.make_async_copy(source, w_buf.at[k * SLOTS + s], w_sem.at[k * SLOTS + s])

        def v_copy(p, s):
            array, column, width = pieces[p]
            source = v_hbm[array].at[pl.ds(s * WIDTH, WIDTH), pl.ds(column, width)]
            return pltpu.make_async_copy(source, v_buf.at[p * SLOTS + s, :, pl.ds(0, width)], v_sem.at[p * SLOTS + s])

        def each(k, s, act):
            if s == 0:
                act()
            else:
                pl.when(s < count[meta[first + k]])(act)

        for k in range(n):
            for s in range(SLOTS):

                def begin(k=k, s=s):
                    w_copy(k, s).start()
                    for p in range(starts[k], starts[k + 1]):
                        v_copy(p, s).start()

                each(k, s, begin)

        core = meta[CORE]
        half = 0
        for k in range(n):
            for p in range(starts[k], starts[k + 1]):
                width = pieces[p][2]
                for s in range(SLOTS):

                    def add(k=k, s=s, p=p, width=width):
                        if p == starts[k]:
                            w_copy(k, s).wait()
                        v_copy(p, s).wait()
                        part = jnp.dot(
                            w_buf[k * SLOTS + s], v_buf[p * SLOTS + s, :, :width], preferred_element_type=F32
                        ).reshape(rows // 32, 2, 16, width)
                        if s == 0:
                            acc_ref[..., :width] = part
                        else:
                            acc_ref[..., :width] += part

                    each(k, s, add)
                for column in range(0, width, HALF):
                    keep_ref[:, half] = acc_ref[:, core, :, column : column + HALF]
                    send_ref[:, half] = acc_ref[:, 1 - core, :, column : column + HALF]
                    half += 1

    out = jax.ShapeDtypeStruct((rows // 32, halves, 16, HALF), F32)
    blank = pl.BlockSpec(memory_space=pl.ANY)
    whole = pl.BlockSpec(memory_space=pltpu.VMEM)
    return pl.pallas_call(
        body,
        out_shape=(out, out),
        grid_spec=pltpu.PrefetchScalarGridSpec(
            num_scalar_prefetch=3,
            in_specs=[blank] * (1 + len(arrays)),
            out_specs=(whole, whole),
            scratch_shapes=[
                pltpu.VMEM((n * SLOTS, rows, WIDTH), walk.dtype),
                pltpu.VMEM((len(pieces) * SLOTS, WIDTH, widest), walk.dtype),
                pltpu.VMEM((rows // 32, 2, 16, widest), F32),
                pltpu.SemaphoreType.DMA((n * SLOTS,)),
                pltpu.SemaphoreType.DMA((len(pieces) * SLOTS,)),
            ],
        ),
    )(*scalars, walk, *arrays)


def squares(meta, ends):
    spots = [(p, half) for p, panel in enumerate(PANELS) for half in panel[2]]

    def body(meta, *refs):
        sq_ref, sum_ref, row_ref = refs[len(ends) :]
        e = 0
        for end in refs[: len(ends)]:
            for j in range(end.shape[0]):
                x = end[j]
                x = x * x
                p, half = spots[e]
                at = pl.multiple_of(meta[p] * WIDTH + half * HALF, HALF)
                sq_ref[:, pl.ds(at, HALF)] = x
                total = jnp.sum(x, axis=0, keepdims=True)
                row_ref[pl.ds(at // 128, 1)] = total[:, :128]
                row_ref[pl.ds(at // 128 + 1, 1)] = total[:, 128:]
                e += 1
        sum_ref[...] = jnp.broadcast_to(row_ref[...][None], sum_ref.shape)

    whole = pl.BlockSpec(memory_space=pltpu.VMEM)
    return pl.pallas_call(
        body,
        out_shape=(jax.ShapeDtypeStruct((16, 4096), F32), jax.ShapeDtypeStruct((16, 32, 128), F32)),
        grid_spec=pltpu.PrefetchScalarGridSpec(
            num_scalar_prefetch=1,
            in_specs=[whole] * len(ends),
            out_specs=(whole, whole),
            scratch_shapes=[pltpu.VMEM((32, 128), F32)],
        ),
        name="squares",
    )(meta, *ends)


def scaled(squared, sums):
    def body(sq_ref, sum_ref, out_ref):
        total = sum_ref[0]
        for t in range(1, sums.shape[0]):
            total = total + sum_ref[t]
        scale = total / 4096 + 1e-06
        for r in range(32):
            at = slice(r * 128, r * 128 + 128)
            out_ref[:, at] = sq_ref[:, at] / scale[r : r + 1]

    return pl.pallas_call(body, out_shape=jax.ShapeDtypeStruct(squared.shape, F32), name="scaled")(squared, sums)


def encode(total):
    peers, n = total.shape[:2]
    top = jnp.max(jnp.abs(total), axis=(0, 2))
    scale = lax.reduce_precision(jnp.maximum(top * (SCALE * 1.002), 6.2e-05), 5, 10)
    t = total * (SCALE / scale)[None, :, None]
    codes = (t * jnp.abs(t) * TOP).astype(WIRE).reshape(peers, n * 16, HALF)
    rows = jnp.pad(scale.astype(WIRE), ((0, 8 - n), (0, 0)))
    return jnp.concatenate([codes, jnp.broadcast_to(rows[None], (peers, 8, HALF))], axis=1)


def decode(coded):
    peers, n = coded.shape[0], (coded.shape[1] - 8) // 16
    codes = coded[:, : n * 16].astype(F32).reshape(peers, n, 16, HALF)
    scale = coded[:, n * 16 : n * 17].astype(F32) * (1 / SCALE)
    size = jnp.sqrt(jnp.abs(codes) * (1 / TOP))
    return jnp.sum(jnp.where(codes < 0, -size, size) * scale[:, :, None], axis=0)


def pipeline(walk, values, col_index, col_count):
    meta = coordinates()
    scalars = (meta, col_index.reshape(-1), col_count.reshape(-1))

    def move(x, **by):
        return send(x, **by)

    def pair(left, right):
        return [(left, 0, HALF), (right, 0, HALF)]

    def one(array):
        return [(array, 0, HALF)]

    ends = []

    def work(batch, given):
        keep, give = product(batch, scalars, walk, given)
        got = move(give, dc=1)
        arrived = lax.all_to_all(encode(keep + got), ("z", "xl"), 0, 0, tiled=True)
        ends.append(decode(arrived))

    own = (values[:, :HALF], values[:, HALF:])
    up = [move(own[t], dy=1) for t in range(2)]
    down = [move(own[t], dy=3) for t in range(2)]
    over = [move(own[t], dxh=1) for t in range(2)]
    far = [move(up[0], dy=1), move(down[1], dy=3)]
    over_up = [move(over[t], dy=1) for t in range(2)]
    over_down = [move(over[t], dy=3) for t in range(2)]
    over_far = [move(far[t], dxh=1) for t in range(2)]

    work(0, [[(values, 0, WIDTH)]])
    work(1, [pair(*up), pair(*down), pair(*over)])
    work(2, [pair(*far), one(over_up[0]), one(over_down[0]), one(over_far[0])])
    work(3, [one(over_up[1]), one(over_down[1]), one(over_far[1])])

    squared, sums = squares(meta, ends)
    sums = jnp.sum(lax.all_to_all(sums, ("z", "core"), 0, 0), axis=0)
    sums = lax.all_to_all(jnp.broadcast_to(sums[None], (16, 32, 128)), ("xh", "y", "xl"), 0, 0)
    return scaled(squared, sums)


def solution(mesh):
    fine = Mesh(mesh.devices.reshape(SIZES), AXES)
    blk, group = ("xh", "y"), ("z", "xl", "core")
    return jax.shard_map(
        pipeline,
        mesh=fine,
        in_specs=(P(blk, group), P(group, blk), P(group, None), P(group, None)),
        out_specs=P((*blk, *group), None),
        check_vma=False,
    )
```

```python
import itertools

import jax
import jax.numpy as jnp
import numpy as np
from jax import lax
from jax.experimental import pallas as pl
from jax.experimental.pallas import tpu as pltpu
from jax.sharding import Mesh
from jax.sharding import PartitionSpec as P


AXES = ("xh", "y", "z", "xl", "core")
SIZES = (2, 4, 8, 2, 2)
SLOTS = 3
WIDTH = 512
HALF = 256
F32 = jnp.float32
WIRE = jnp.float16
TOP = 60000.0
SCALE = 64.0

BATCHES = (
    ((0, 0, (0, 1)),),
    ((0, 3, (0, 1)), (0, 1, (0, 1)), (1, 0, (0, 1))),
    ((0, 2, (0, 1)),),
    ((1, 3, (0, 1)), (1, 1, (0, 1)), (1, 2, (0, 1))),
)
PANELS = tuple(itertools.chain(*BATCHES))
CORE, XLO = len(PANELS), len(PANELS) + 1


def moves(dxh=0, dy=0, dz=0, dxl=0, dc=0):
    pairs = []
    for at in itertools.product(*(range(n) for n in SIZES)):
        to = [(a + d) % n for a, d, n in zip(at, (dxh, dy, dz, dxl, dc), SIZES)]
        pairs.append((int(np.ravel_multi_index(at, SIZES)), int(np.ravel_multi_index(to, SIZES))))
    return pairs


def send(x, **by):
    return lax.ppermute(x, AXES, moves(**by))


def coordinates():
    dx = np.array([p[0] for p in PANELS] + [0, 0], np.int32)
    dy = np.array([p[1] for p in PANELS] + [0, 0], np.int32)
    spot = np.arange(len(dx), dtype=np.int32)
    xh, y, xl, core = (lax.axis_index(name).astype(jnp.int32) for name in ("xh", "y", "xl", "core"))
    panels = ((xh ^ dx) * 4 + ((y + dy) & 3)) * (spot < CORE).astype(np.int32)
    return panels + core * (spot == CORE) + xl * (spot == XLO)


def product(batch, scalars, walk, values, both):
    panels = BATCHES[batch]
    first = sum(len(b) for b in BATCHES[:batch])
    rows = walk.shape[0]
    arrays = []
    pieces = []
    for given in values:
        for array, column, width in given:
            known = [i for i, a in enumerate(arrays) if a is array]
            if not known:
                arrays.append(array)
            pieces.append((known[0] if known else len(arrays) - 1, column, width))
    per_panel = [len(given) for given in values]
    starts = np.cumsum([0] + per_panel)
    halves = sum(p[2] for p in pieces) // HALF
    widest = max(p[2] for p in pieces)
    n = len(panels)

    def body(meta, index, count, w_hbm, *refs):
        v_hbm = refs[: len(arrays)]
        keep_ref, send_ref, w_buf, v_buf, acc_ref, w_sem, v_sem = refs[len(arrays) :]

        def w_copy(k, s):
            block = index[s * 8 + meta[first + k]]
            source = w_hbm.at[:, pl.ds(pl.multiple_of(block * WIDTH, WIDTH), WIDTH)]
            return pltpu.make_async_copy(source, w_buf.at[k * SLOTS + s], w_sem.at[k * SLOTS + s])

        def v_copy(p, s):
            array, column, width = pieces[p]
            source = v_hbm[array].at[pl.ds(s * WIDTH, WIDTH), pl.ds(column, width)]
            return pltpu.make_async_copy(source, v_buf.at[p * SLOTS + s, :, pl.ds(0, width)], v_sem.at[p * SLOTS + s])

        def each(k, s, act):
            if s == 0:
                act()
            else:
                pl.when(s < count[meta[first + k]])(act)

        for k in range(n):
            for s in range(SLOTS):

                def begin(k=k, s=s):
                    w_copy(k, s).start()
                    for p in range(starts[k], starts[k + 1]):
                        v_copy(p, s).start()

                each(k, s, begin)

        core, xl = meta[CORE], meta[XLO]
        half = 0
        for k in range(n):
            for p in range(starts[k], starts[k + 1]):
                width = pieces[p][2]
                for s in range(SLOTS):

                    def add(k=k, s=s, p=p, width=width):
                        if p == starts[k]:
                            w_copy(k, s).wait()
                        v_copy(p, s).wait()
                        part = jnp.dot(
                            w_buf[k * SLOTS + s], v_buf[p * SLOTS + s, :, :width], preferred_element_type=F32
                        ).reshape(rows // 64, 2, 2, 16, width)
                        if s == 0:
                            acc_ref[..., :width] = part
                        else:
                            acc_ref[..., :width] += part

                    each(k, s, add)
                for column in range(0, width, HALF):
                    for r, at in ((0, 0), (1, 1)) if both else ((0, xl), (1, 1 - xl)):
                        keep_ref[:, r, half] = acc_ref[:, at, core, :, column : column + HALF]
                        send_ref[:, r, half] = acc_ref[:, at, 1 - core, :, column : column + HALF]
                    half += 1

    out = jax.ShapeDtypeStruct((rows // 64, 2, halves, 16, HALF), F32)
    blank = pl.BlockSpec(memory_space=pl.ANY)
    whole = pl.BlockSpec(memory_space=pltpu.VMEM)
    return pl.pallas_call(
        body,
        out_shape=(out, out),
        grid_spec=pltpu.PrefetchScalarGridSpec(
            num_scalar_prefetch=3,
            in_specs=[blank] * (1 + len(arrays)),
            out_specs=(whole, whole),
            scratch_shapes=[
                pltpu.VMEM((n * SLOTS, rows, WIDTH), walk.dtype),
                pltpu.VMEM((len(pieces) * SLOTS, WIDTH, widest), walk.dtype),
                pltpu.VMEM((rows // 64, 2, 2, 16, widest), F32),
                pltpu.SemaphoreType.DMA((n * SLOTS,)),
                pltpu.SemaphoreType.DMA((len(pieces) * SLOTS,)),
            ],
        ),
    )(*scalars, walk, *arrays)


def squares(meta, ends):
    spots = [(p, half) for p, panel in enumerate(PANELS) for half in panel[2]]
    terms = [len(end) for end in ends]

    def body(meta, *refs):
        sq_ref, sum_ref, row_ref = refs[sum(terms) :]
        e = first = 0
        for m in terms:
            for j in range(refs[first].shape[0]):
                x = refs[first][j]
                for k in range(1, m):
                    x = x + refs[first + k][j]
                x = x * x
                p, half = spots[e]
                at = pl.multiple_of(meta[p] * WIDTH + half * HALF, HALF)
                sq_ref[:, pl.ds(at, HALF)] = x
                total = jnp.sum(x, axis=0, keepdims=True)
                row_ref[pl.ds(at // 128, 1)] = total[:, :128]
                row_ref[pl.ds(at // 128 + 1, 1)] = total[:, 128:]
                e += 1
            first += m
        sum_ref[...] = jnp.broadcast_to(row_ref[...][None], sum_ref.shape)

    whole = pl.BlockSpec(memory_space=pltpu.VMEM)
    return pl.pallas_call(
        body,
        out_shape=(jax.ShapeDtypeStruct((16, 4096), F32), jax.ShapeDtypeStruct((16, 32, 128), F32)),
        grid_spec=pltpu.PrefetchScalarGridSpec(
            num_scalar_prefetch=1,
            in_specs=[whole] * sum(terms),
            out_specs=(whole, whole),
            scratch_shapes=[pltpu.VMEM((32, 128), F32)],
        ),
        name="squares",
    )(meta, *itertools.chain(*ends))


def scaled(squared, sums):
    def body(sq_ref, sum_ref, out_ref):
        total = sum_ref[0]
        for t in range(1, sums.shape[0]):
            total = total + sum_ref[t]
        scale = total / 4096 + 1e-06
        for r in range(32):
            at = slice(r * 128, r * 128 + 128)
            out_ref[:, at] = sq_ref[:, at] / scale[r : r + 1]

    return pl.pallas_call(body, out_shape=jax.ShapeDtypeStruct(squared.shape, F32), name="scaled")(squared, sums)


def encode(total):
    peers, n = total.shape[0], total.shape[-3]
    top = jnp.max(jnp.abs(total), axis=(*range(total.ndim - 3), total.ndim - 2))
    scale = lax.reduce_precision(jnp.maximum(top * (SCALE * 1.002), 6.2e-05), 5, 10)
    t = total * (SCALE / scale)[:, None]
    codes = (t * jnp.abs(t) * TOP).astype(WIRE).reshape(peers, -1, HALF)
    rows = jnp.pad(scale.astype(WIRE), ((0, 8 - n), (0, 0)))
    return jnp.concatenate([codes, jnp.broadcast_to(rows[None], (peers, 8, HALF))], axis=1)


def decode(coded, shape):
    peers, end = coded.shape[0], coded.shape[1] - 8
    codes = coded[:, :end].astype(F32).reshape(peers, *shape)
    scale = coded[:, end : end + shape[-3]].astype(F32) * (1 / SCALE)
    scale = scale.reshape(peers, *([1] * (len(shape) - 3)), shape[-3], 1, HALF)
    size = jnp.sqrt(jnp.abs(codes) * (1 / TOP))
    return jnp.sum(jnp.where(codes < 0, -size, size) * scale, axis=0)


def pipeline(walk, values, col_index, col_count):
    meta = coordinates()
    scalars = (meta, col_index.reshape(-1), col_count.reshape(-1))

    def move(x, **by):
        return send(x, **by)

    def whole(array):
        return [(array, 0, WIDTH)]

    def pair(left, right):
        return [(left, 0, HALF), (right, 0, HALF)]

    ends = []

    def work(batch, given, both=False):
        keep, give = product(batch, scalars, walk, given, both)
        got = move(give, dc=1)
        n = keep.shape[2]
        if both:
            coded = encode((keep + got).reshape(16, n, 16, HALF))
            arrived = lax.all_to_all(coded, ("z", "xl"), 0, 0, tiled=True)
            ends.append((decode(arrived, (n, 16, HALF)),))
        else:
            arrived = lax.all_to_all(encode(keep + got), "z", 0, 0, tiled=True)
            total = decode(arrived, (2, n, 16, HALF))
            ends.append((total[0], move(total[1], dxl=1)))

    up = move(values, dy=1)
    down = move(values, dy=3)
    over = move(values, dxh=1)
    far = [move(up[:, :HALF], dy=1), move(down[:, HALF:], dy=3)]
    over_up = move(over, dy=1)
    over_down = move(over, dy=3)
    over_far = [move(far[t], dxh=1) for t in range(2)]

    work(0, [whole(values)])
    work(1, [whole(up), whole(down), whole(over)])
    work(2, [pair(*far)])
    work(3, [whole(over_up), whole(over_down), pair(*over_far)], both=True)

    squared, sums = squares(meta, ends)
    sums = jnp.sum(lax.all_to_all(sums, ("z", "xl"), 0, 0), axis=0)
    sums = lax.all_to_all(jnp.broadcast_to(sums[None], (16, 32, 128)), ("xh", "y", "core"), 0, 0)
    return scaled(squared, sums)


def solution(mesh):
    fine = Mesh(mesh.devices.reshape(SIZES), AXES)
    blk, group = ("xh", "y"), ("z", "xl", "core")
    return jax.shard_map(
        pipeline,
        mesh=fine,
        in_specs=(P(blk, group), P(group, blk), P(group, None), P(group, None)),
        out_specs=P((*blk, *group), None),
        check_vma=False,
    )
```

```python
import itertools

import jax
import jax.numpy as jnp
import numpy as np
from jax import lax
from jax.experimental import pallas as pl
from jax.experimental.pallas import tpu as pltpu
from jax.sharding import Mesh
from jax.sharding import PartitionSpec as P


AXES = ("xh", "y", "z", "xl", "core")
SIZES = (2, 4, 8, 2, 2)
SLOTS = 3
WIDTH = 512
HALF = 256
F32 = jnp.float32
WIRE = jnp.float16
TOP = 60000.0
SCALE = 64.0

BATCHES = (
    ((0, 0, (0, 1)), (0, 3, (0,)), (0, 1, (0,))),
    ((0, 3, (1,)), (0, 1, (1,)), (1, 0, (0, 1))),
    ((0, 2, (0, 1)),),
    ((1, 3, (0,)), (1, 1, (0,)), (1, 2, (0,))),
    ((1, 3, (1,)), (1, 1, (1,)), (1, 2, (1,))),
)
PANELS = tuple(itertools.chain(*BATCHES))
CORE, XLO = len(PANELS), len(PANELS) + 1


def moves(dxh=0, dy=0, dz=0, dxl=0, dc=0):
    pairs = []
    for at in itertools.product(*(range(n) for n in SIZES)):
        to = [(a + d) % n for a, d, n in zip(at, (dxh, dy, dz, dxl, dc), SIZES)]
        pairs.append((int(np.ravel_multi_index(at, SIZES)), int(np.ravel_multi_index(to, SIZES))))
    return pairs


def send(x, **by):
    return lax.ppermute(x, AXES, moves(**by))


def coordinates():
    dx = np.array([p[0] for p in PANELS] + [0, 0], np.int32)
    dy = np.array([p[1] for p in PANELS] + [0, 0], np.int32)
    spot = np.arange(len(dx), dtype=np.int32)
    xh, y, xl, core = (lax.axis_index(name).astype(jnp.int32) for name in ("xh", "y", "xl", "core"))
    panels = ((xh ^ dx) * 4 + ((y + dy) & 3)) * (spot < CORE).astype(np.int32)
    return panels + core * (spot == CORE) + xl * (spot == XLO)


def product(batch, scalars, walk, values, both):
    panels = BATCHES[batch]
    first = sum(len(b) for b in BATCHES[:batch])
    rows = walk.shape[0]
    arrays = []
    pieces = []
    for given in values:
        for array, column, width in given:
            known = [i for i, a in enumerate(arrays) if a is array]
            if not known:
                arrays.append(array)
            pieces.append((known[0] if known else len(arrays) - 1, column, width))
    per_panel = [len(given) for given in values]
    starts = np.cumsum([0] + per_panel)
    halves = sum(p[2] for p in pieces) // HALF
    widest = max(p[2] for p in pieces)
    n = len(panels)

    def body(meta, index, count, w_hbm, *refs):
        v_hbm = refs[: len(arrays)]
        keep_ref, send_ref, w_buf, v_buf, acc_ref, w_sem, v_sem = refs[len(arrays) :]

        def w_copy(k, s):
            block = index[s * 8 + meta[first + k]]
            source = w_hbm.at[:, pl.ds(pl.multiple_of(block * WIDTH, WIDTH), WIDTH)]
            return pltpu.make_async_copy(source, w_buf.at[k * SLOTS + s], w_sem.at[k * SLOTS + s])

        def v_copy(p, s):
            array, column, width = pieces[p]
            source = v_hbm[array].at[pl.ds(s * WIDTH, WIDTH), pl.ds(column, width)]
            return pltpu.make_async_copy(source, v_buf.at[p * SLOTS + s, :, pl.ds(0, width)], v_sem.at[p * SLOTS + s])

        def each(k, s, act):
            if s == 0:
                act()
            else:
                pl.when(s < count[meta[first + k]])(act)

        for k in range(n):
            for s in range(SLOTS):

                def begin(k=k, s=s):
                    w_copy(k, s).start()
                    for p in range(starts[k], starts[k + 1]):
                        v_copy(p, s).start()

                each(k, s, begin)

        core, xl = meta[CORE], meta[XLO]
        half = 0
        for k in range(n):
            for p in range(starts[k], starts[k + 1]):
                width = pieces[p][2]
                for s in range(SLOTS):

                    def add(k=k, s=s, p=p, width=width):
                        if p == starts[k]:
                            w_copy(k, s).wait()
                        v_copy(p, s).wait()
                        part = jnp.dot(
                            w_buf[k * SLOTS + s], v_buf[p * SLOTS + s, :, :width], preferred_element_type=F32
                        ).reshape(rows // 64, 2, 2, 16, width)
                        if s == 0:
                            acc_ref[..., :width] = part
                        else:
                            acc_ref[..., :width] += part

                    each(k, s, add)
                for column in range(0, width, HALF):
                    for r, at in ((0, 0), (1, 1)) if both else ((0, xl), (1, 1 - xl)):
                        keep_ref[:, r, half] = acc_ref[:, at, core, :, column : column + HALF]
                        send_ref[:, r, half] = acc_ref[:, at, 1 - core, :, column : column + HALF]
                    half += 1

    out = jax.ShapeDtypeStruct((rows // 64, 2, halves, 16, HALF), F32)
    blank = pl.BlockSpec(memory_space=pl.ANY)
    whole = pl.BlockSpec(memory_space=pltpu.VMEM)
    return pl.pallas_call(
        body,
        out_shape=(out, out),
        grid_spec=pltpu.PrefetchScalarGridSpec(
            num_scalar_prefetch=3,
            in_specs=[blank] * (1 + len(arrays)),
            out_specs=(whole, whole),
            scratch_shapes=[
                pltpu.VMEM((n * SLOTS, rows, WIDTH), walk.dtype),
                pltpu.VMEM((len(pieces) * SLOTS, WIDTH, widest), walk.dtype),
                pltpu.VMEM((rows // 64, 2, 2, 16, widest), F32),
                pltpu.SemaphoreType.DMA((n * SLOTS,)),
                pltpu.SemaphoreType.DMA((len(pieces) * SLOTS,)),
            ],
        ),
    )(*scalars, walk, *arrays)


def squares(meta, ends):
    spots = [(p, half) for p, panel in enumerate(PANELS) for half in panel[2]]
    terms = [len(end) for end in ends]

    def body(meta, *refs):
        sq_ref, sum_ref, row_ref = refs[sum(terms) :]
        e = first = 0
        for m in terms:
            for j in range(refs[first].shape[0]):
                x = refs[first][j]
                for k in range(1, m):
                    x = x + refs[first + k][j]
                x = x * x
                p, half = spots[e]
                at = pl.multiple_of(meta[p] * WIDTH + half * HALF, HALF)
                sq_ref[:, pl.ds(at, HALF)] = x
                total = jnp.sum(x, axis=0, keepdims=True)
                row_ref[pl.ds(at // 128, 1)] = total[:, :128]
                row_ref[pl.ds(at // 128 + 1, 1)] = total[:, 128:]
                e += 1
            first += m
        sum_ref[...] = jnp.broadcast_to(row_ref[...][None], sum_ref.shape)

    whole = pl.BlockSpec(memory_space=pltpu.VMEM)
    return pl.pallas_call(
        body,
        out_shape=(jax.ShapeDtypeStruct((16, 4096), F32), jax.ShapeDtypeStruct((16, 32, 128), F32)),
        grid_spec=pltpu.PrefetchScalarGridSpec(
            num_scalar_prefetch=1,
            in_specs=[whole] * sum(terms),
            out_specs=(whole, whole),
            scratch_shapes=[pltpu.VMEM((32, 128), F32)],
        ),
        name="squares",
    )(meta, *itertools.chain(*ends))


def scaled(squared, sums):
    def body(sq_ref, sum_ref, out_ref):
        total = sum_ref[0]
        for t in range(1, sums.shape[0]):
            total = total + sum_ref[t]
        scale = total / 4096 + 1e-06
        for r in range(32):
            at = slice(r * 128, r * 128 + 128)
            out_ref[:, at] = sq_ref[:, at] / scale[r : r + 1]

    return pl.pallas_call(body, out_shape=jax.ShapeDtypeStruct(squared.shape, F32), name="scaled")(squared, sums)


def encode(total):
    peers, n = total.shape[0], total.shape[-3]
    top = jnp.max(jnp.abs(total), axis=(*range(total.ndim - 3), total.ndim - 2))
    scale = lax.reduce_precision(jnp.maximum(top * (SCALE * 1.002), 6.2e-05), 5, 10)
    t = total * (SCALE / scale)[:, None]
    codes = (t * jnp.abs(t) * TOP).astype(WIRE).reshape(peers, -1, HALF)
    rows = jnp.pad(scale.astype(WIRE), ((0, 8 - n), (0, 0)))
    return jnp.concatenate([codes, jnp.broadcast_to(rows[None], (peers, 8, HALF))], axis=1)


def decode(coded, shape):
    peers, end = coded.shape[0], coded.shape[1] - 8
    codes = coded[:, :end].astype(F32).reshape(peers, *shape)
    scale = coded[:, end : end + shape[-3]].astype(F32) * (1 / SCALE)
    scale = scale.reshape(peers, *([1] * (len(shape) - 3)), shape[-3], 1, HALF)
    size = jnp.sqrt(jnp.abs(codes) * (1 / TOP))
    return jnp.sum(jnp.where(codes < 0, -size, size) * scale, axis=0)


def pipeline(walk, values, col_index, col_count):
    meta = coordinates()
    scalars = (meta, col_index.reshape(-1), col_count.reshape(-1))

    def move(x, **by):
        return send(x, **by)

    def whole(array):
        return [(array, 0, WIDTH)]

    def pair(left, right):
        return [(left, 0, HALF), (right, 0, HALF)]

    def one(array):
        return [(array, 0, HALF)]

    ends = []

    def work(batch, given, both=False):
        keep, give = product(batch, scalars, walk, given, both)
        got = move(give, dc=1)
        n = keep.shape[2]
        if both:
            coded = encode((keep + got).reshape(16, n, 16, HALF))
            arrived = lax.all_to_all(coded, ("z", "xl"), 0, 0, tiled=True)
            ends.append((decode(arrived, (n, 16, HALF)),))
        else:
            arrived = lax.all_to_all(encode(keep + got), "z", 0, 0, tiled=True)
            total = decode(arrived, (2, n, 16, HALF))
            ends.append((total[0], move(total[1], dxl=1)))

    own = (values[:, :HALF], values[:, HALF:])
    up = [move(own[t], dy=1) for t in range(2)]
    down = [move(own[t], dy=3) for t in range(2)]
    over = [move(own[t], dxh=1) for t in range(2)]
    far = [move(up[0], dy=1), move(down[1], dy=3)]
    over_up = [move(over[t], dy=1) for t in range(2)]
    over_down = [move(over[t], dy=3) for t in range(2)]
    over_far = [move(far[t], dxh=1) for t in range(2)]

    work(0, [whole(values), one(up[0]), one(down[0])])
    work(1, [one(up[1]), one(down[1]), pair(*over)])
    work(2, [pair(*far)])
    work(3, [one(over_up[0]), one(over_down[0]), one(over_far[0])])
    work(4, [one(over_up[1]), one(over_down[1]), one(over_far[1])], both=True)

    squared, sums = squares(meta, ends)
    sums = jnp.sum(lax.all_to_all(sums, ("z", "xl"), 0, 0), axis=0)
    sums = lax.all_to_all(jnp.broadcast_to(sums[None], (16, 32, 128)), ("xh", "y", "core"), 0, 0)
    return scaled(squared, sums)


def solution(mesh):
    fine = Mesh(mesh.devices.reshape(SIZES), AXES)
    blk, group = ("xh", "y"), ("z", "xl", "core")
    return jax.shard_map(
        pipeline,
        mesh=fine,
        in_specs=(P(blk, group), P(group, blk), P(group, None), P(group, None)),
        out_specs=P((*blk, *group), None),
        check_vma=False,
    )
```

```python
import itertools
import math

import jax
import jax.numpy as jnp
import numpy as np
from jax import lax
from jax.experimental import pallas as pl
from jax.experimental.pallas import tpu as pltpu
from jax.sharding import Mesh
from jax.sharding import PartitionSpec as P


AXES = ("xh", "y", "z", "xl", "core")
SIZES = (2, 4, 8, 2, 2)
SLOTS = 3
WIDTH = 512
HALF = 256
F32 = jnp.float32
WIRE = jnp.float16
TOP = 60000.0
SCALE = 64.0

BATCHES = (
    ((0, 0, (0, 1)),),
    ((0, 3, (0, 1)), (0, 1, (0, 1)), (1, 0, (0, 1))),
    ((1, 3, (0,)), (1, 1, (0,)), (1, 2, (0,))),
    ((0, 2, (0, 1)),),
    ((1, 3, (1,)), (1, 1, (1,)), (1, 2, (1,))),
)
PANELS = tuple(itertools.chain(*BATCHES))
CORE, XLO = len(PANELS), len(PANELS) + 1


def moves(dxh=0, dy=0, dz=0, dxl=0, dc=0):
    pairs = []
    for at in itertools.product(*(range(n) for n in SIZES)):
        to = [(a + d) % n for a, d, n in zip(at, (dxh, dy, dz, dxl, dc), SIZES)]
        pairs.append((int(np.ravel_multi_index(at, SIZES)), int(np.ravel_multi_index(to, SIZES))))
    return pairs


def send(x, **by):
    return lax.ppermute(x, AXES, moves(**by))


def coordinates():
    dx = np.array([p[0] for p in PANELS] + [0, 0], np.int32)
    dy = np.array([p[1] for p in PANELS] + [0, 0], np.int32)
    spot = np.arange(len(dx), dtype=np.int32)
    xh, y, xl, core = (lax.axis_index(name).astype(jnp.int32) for name in ("xh", "y", "xl", "core"))
    panels = ((xh ^ dx) * 4 + ((y + dy) & 3)) * (spot < CORE).astype(np.int32)
    return panels + core * (spot == CORE) + xl * (spot == XLO)


def product(batch, scalars, walk, values, both):
    panels = BATCHES[batch]
    first = sum(len(b) for b in BATCHES[:batch])
    rows = walk.shape[0]
    arrays = []
    pieces = []
    for given in values:
        for array, column, width in given:
            known = [i for i, a in enumerate(arrays) if a is array]
            if not known:
                arrays.append(array)
            pieces.append((known[0] if known else len(arrays) - 1, column, width))
    per_panel = [len(given) for given in values]
    starts = np.cumsum([0] + per_panel)
    halves = sum(p[2] for p in pieces) // HALF
    widest = max(p[2] for p in pieces)
    n = len(panels)

    def body(meta, index, count, w_hbm, *refs):
        v_hbm = refs[: len(arrays)]
        keep_ref, send_ref, w_buf, v_buf, acc_ref, w_sem, v_sem = refs[len(arrays) :]

        def w_copy(k, s):
            block = index[s * 8 + meta[first + k]]
            source = w_hbm.at[:, pl.ds(pl.multiple_of(block * WIDTH, WIDTH), WIDTH)]
            return pltpu.make_async_copy(source, w_buf.at[k * SLOTS + s], w_sem.at[k * SLOTS + s])

        def v_copy(p, s):
            array, column, width = pieces[p]
            source = v_hbm[array].at[pl.ds(s * WIDTH, WIDTH), pl.ds(column, width)]
            return pltpu.make_async_copy(source, v_buf.at[p * SLOTS + s, :, pl.ds(0, width)], v_sem.at[p * SLOTS + s])

        def each(k, s, act):
            if s == 0:
                act()
            else:
                pl.when(s < count[meta[first + k]])(act)

        for k in range(n):
            for s in range(SLOTS):

                def begin(k=k, s=s):
                    w_copy(k, s).start()
                    for p in range(starts[k], starts[k + 1]):
                        v_copy(p, s).start()

                each(k, s, begin)

        core, xl = meta[CORE], meta[XLO]
        half = 0
        for k in range(n):
            for p in range(starts[k], starts[k + 1]):
                width = pieces[p][2]
                for s in range(SLOTS):

                    def add(k=k, s=s, p=p, width=width):
                        if p == starts[k]:
                            w_copy(k, s).wait()
                        v_copy(p, s).wait()
                        part = jnp.dot(
                            w_buf[k * SLOTS + s], v_buf[p * SLOTS + s, :, :width], preferred_element_type=F32
                        ).reshape(rows // 64, 2, 2, 16, width)
                        if s == 0:
                            acc_ref[..., :width] = part
                        else:
                            acc_ref[..., :width] += part

                    each(k, s, add)
                for column in range(0, width, HALF):
                    for r, at in ((0, 0), (1, 1)) if both else ((0, xl), (1, 1 - xl)):
                        keep_ref[:, r, half] = acc_ref[:, at, core, :, column : column + HALF]
                        send_ref[:, r, half] = acc_ref[:, at, 1 - core, :, column : column + HALF]
                    half += 1

    out = jax.ShapeDtypeStruct((rows // 64, 2, halves, 16, HALF), F32)
    blank = pl.BlockSpec(memory_space=pl.ANY)
    whole = pl.BlockSpec(memory_space=pltpu.VMEM)
    return pl.pallas_call(
        body,
        out_shape=(out, out),
        grid_spec=pltpu.PrefetchScalarGridSpec(
            num_scalar_prefetch=3,
            in_specs=[blank] * (1 + len(arrays)),
            out_specs=(whole, whole),
            scratch_shapes=[
                pltpu.VMEM((n * SLOTS, rows, WIDTH), walk.dtype),
                pltpu.VMEM((len(pieces) * SLOTS, WIDTH, widest), walk.dtype),
                pltpu.VMEM((rows // 64, 2, 2, 16, widest), F32),
                pltpu.SemaphoreType.DMA((n * SLOTS,)),
                pltpu.SemaphoreType.DMA((len(pieces) * SLOTS,)),
            ],
        ),
    )(*scalars, walk, *arrays)


def squares(meta, ends):
    spots = [(p, half) for p, panel in enumerate(PANELS) for half in panel[2]]
    terms = [len(end) for end in ends]

    def body(meta, *refs):
        sq_ref, sum_ref, row_ref = refs[sum(terms) :]
        e = first = 0
        for m in terms:
            for j in range(refs[first].shape[0]):
                x = refs[first][j]
                for k in range(1, m):
                    x = x + refs[first + k][j]
                x = x * x
                p, half = spots[e]
                at = pl.multiple_of(meta[p] * WIDTH + half * HALF, HALF)
                sq_ref[:, pl.ds(at, HALF)] = x
                total = jnp.sum(x, axis=0, keepdims=True)
                row_ref[pl.ds(at // 128, 1)] = total[:, :128]
                row_ref[pl.ds(at // 128 + 1, 1)] = total[:, 128:]
                e += 1
            first += m
        sum_ref[...] = jnp.broadcast_to(row_ref[...][None], sum_ref.shape)

    whole = pl.BlockSpec(memory_space=pltpu.VMEM)
    return pl.pallas_call(
        body,
        out_shape=(jax.ShapeDtypeStruct((16, 4096), F32), jax.ShapeDtypeStruct((16, 32, 128), F32)),
        grid_spec=pltpu.PrefetchScalarGridSpec(
            num_scalar_prefetch=1,
            in_specs=[whole] * sum(terms),
            out_specs=(whole, whole),
            scratch_shapes=[pltpu.VMEM((32, 128), F32)],
        ),
        name="squares",
    )(meta, *itertools.chain(*ends))


def scaled(squared, sums):
    def body(sq_ref, sum_ref, out_ref):
        total = sum_ref[0]
        for t in range(1, sums.shape[0]):
            total = total + sum_ref[t]
        scale = total / 4096 + 1e-06
        for r in range(32):
            at = slice(r * 128, r * 128 + 128)
            out_ref[:, at] = sq_ref[:, at] / scale[r : r + 1]

    return pl.pallas_call(body, out_shape=jax.ShapeDtypeStruct(squared.shape, F32), name="scaled")(squared, sums)


def encode(totals):
    peers = totals[0].shape[0]
    codes, scales = [], []
    for total in totals:
        top = jnp.max(jnp.abs(total), axis=(*range(total.ndim - 3), total.ndim - 2))
        scale = lax.reduce_precision(jnp.maximum(top * (SCALE * 1.002), 6.2e-05), 5, 10)
        t = total * (SCALE / scale)[:, None]
        codes.append((t * jnp.abs(t) * TOP).astype(WIRE).reshape(peers, -1, HALF))
        scales.append(scale.astype(WIRE))
    rows = jnp.concatenate(scales)
    rows = jnp.pad(rows, ((0, 8 - rows.shape[0]), (0, 0)))
    return jnp.concatenate([*codes, jnp.broadcast_to(rows[None], (peers, 8, HALF))], axis=1)


def decode(coded, shapes):
    peers, end = coded.shape[0], coded.shape[1] - 8
    row, spot, sums = 0, end, []
    for shape in shapes:
        rows, n = math.prod(shape[:-1]), shape[-3]
        codes = coded[:, row : row + rows].astype(F32).reshape(peers, *shape)
        scale = coded[:, spot : spot + n].astype(F32) * (1 / SCALE)
        scale = scale.reshape(peers, *([1] * (len(shape) - 3)), n, 1, HALF)
        size = jnp.sqrt(jnp.abs(codes) * (1 / TOP))
        sums.append(jnp.sum(jnp.where(codes < 0, -size, size) * scale, axis=0))
        row, spot = row + rows, spot + n
    return sums


def pipeline(walk, values, col_index, col_count):
    meta = coordinates()
    scalars = (meta, col_index.reshape(-1), col_count.reshape(-1))

    def move(x, **by):
        return send(x, **by)

    def whole(array):
        return [(array, 0, WIDTH)]

    def pair(left, right):
        return [(left, 0, HALF), (right, 0, HALF)]

    def one(array):
        return [(array, 0, HALF)]

    ends = []

    def partial(batch, given, both=False):
        keep, give = product(batch, scalars, walk, given, both)
        return keep + move(give, dc=1)

    def exchange(totals, both=False):
        if both:
            totals = [t.reshape(16, *t.shape[2:]) for t in totals]
        arrived = lax.all_to_all(encode(totals), ("z", "xl") if both else "z", 0, 0, tiled=True)
        sums = decode(arrived, [t.shape[1:] for t in totals])
        for total in sums:
            ends.append((total,) if both else (total[0], move(total[1], dxl=1)))

    up = move(values, dy=1)
    down = move(values, dy=3)
    over = move(values, dxh=1)
    far = [move(up[:, :HALF], dy=1), move(down[:, HALF:], dy=3)]
    over_half = (over[:, :HALF], over[:, HALF:])
    over_up = [move(over_half[t], dy=1) for t in range(2)]
    over_down = [move(over_half[t], dy=3) for t in range(2)]
    over_far = [move(far[t], dxh=1) for t in range(2)]

    exchange([partial(0, [whole(values)])])
    exchange([partial(1, [whole(up), whole(down), whole(over)])])
    exchange([partial(2, [one(over_up[0]), one(over_down[0]), one(over_far[0])])])
    last = [partial(3, [pair(*far)], both=True)]
    last.append(partial(4, [one(over_up[1]), one(over_down[1]), one(over_far[1])], both=True))
    exchange(last, both=True)

    squared, sums = squares(meta, ends)
    sums = jnp.sum(lax.all_to_all(sums, ("z", "xl"), 0, 0), axis=0)
    sums = lax.all_to_all(jnp.broadcast_to(sums[None], (16, 32, 128)), ("xh", "y", "core"), 0, 0)
    return scaled(squared, sums)


def solution(mesh):
    fine = Mesh(mesh.devices.reshape(SIZES), AXES)
    blk, group = ("xh", "y"), ("z", "xl", "core")
    return jax.shard_map(
        pipeline,
        mesh=fine,
        in_specs=(P(blk, group), P(group, blk), P(group, None), P(group, None)),
        out_specs=P((*blk, *group), None),
        check_vma=False,
    )
```

```python
import itertools
import math

import jax
import jax.numpy as jnp
import numpy as np
from jax import lax
from jax.experimental import pallas as pl
from jax.experimental.pallas import tpu as pltpu
from jax.sharding import Mesh
from jax.sharding import PartitionSpec as P


AXES = ("xh", "y", "z", "xl", "core")
SIZES = (2, 4, 8, 2, 2)
SLOTS = 3
WIDTH = 512
HALF = 256
F32 = jnp.float32
WIRE = jnp.float16
TOP = 60000.0
SCALE = 64.0

BATCHES = (
    ((0, 0, (0, 1)),),
    ((0, 3, (0, 1)), (0, 1, (0, 1)), (1, 0, (0, 1))),
    ((1, 3, (0,)), (1, 1, (0,)), (1, 2, (0,))),
    ((0, 2, (0, 1)),),
    ((1, 3, (1,)), (1, 1, (1,)), (1, 2, (1,))),
)
PANELS = tuple(itertools.chain(*BATCHES))
CORE, XLO = len(PANELS), len(PANELS) + 1


def moves(dxh=0, dy=0, dz=0, dxl=0, dc=0):
    pairs = []
    for at in itertools.product(*(range(n) for n in SIZES)):
        to = [(a + d) % n for a, d, n in zip(at, (dxh, dy, dz, dxl, dc), SIZES)]
        pairs.append((int(np.ravel_multi_index(at, SIZES)), int(np.ravel_multi_index(to, SIZES))))
    return pairs


def send(x, **by):
    return lax.ppermute(x, AXES, moves(**by))


def coordinates():
    dx = np.array([p[0] for p in PANELS] + [0, 0], np.int32)
    dy = np.array([p[1] for p in PANELS] + [0, 0], np.int32)
    spot = np.arange(len(dx), dtype=np.int32)
    xh, y, xl, core = (lax.axis_index(name).astype(jnp.int32) for name in ("xh", "y", "xl", "core"))
    panels = ((xh ^ dx) * 4 + ((y + dy) & 3)) * (spot < CORE).astype(np.int32)
    return panels + core * (spot == CORE) + xl * (spot == XLO)


def product(batch, scalars, walk, values, both):
    panels = BATCHES[batch]
    first = sum(len(b) for b in BATCHES[:batch])
    rows = walk.shape[0]
    arrays = []
    pieces = []
    for given in values:
        for array, column, width in given:
            known = [i for i, a in enumerate(arrays) if a is array]
            if not known:
                arrays.append(array)
            pieces.append((known[0] if known else len(arrays) - 1, column, width))
    per_panel = [len(given) for given in values]
    starts = np.cumsum([0] + per_panel)
    halves = sum(p[2] for p in pieces) // HALF
    widest = max(p[2] for p in pieces)
    n = len(panels)

    def body(meta, index, count, w_hbm, *refs):
        v_hbm = refs[: len(arrays)]
        keep_ref, send_ref, w_buf, v_buf, acc_ref, w_sem, v_sem = refs[len(arrays) :]

        def w_copy(k, s):
            block = index[s * 8 + meta[first + k]]
            source = w_hbm.at[:, pl.ds(pl.multiple_of(block * WIDTH, WIDTH), WIDTH)]
            return pltpu.make_async_copy(source, w_buf.at[k * SLOTS + s], w_sem.at[k * SLOTS + s])

        def v_copy(p, s):
            array, column, width = pieces[p]
            source = v_hbm[array].at[pl.ds(s * WIDTH, WIDTH), pl.ds(column, width)]
            return pltpu.make_async_copy(source, v_buf.at[p * SLOTS + s, :, pl.ds(0, width)], v_sem.at[p * SLOTS + s])

        def each(k, s, act):
            if s == 0:
                act()
            else:
                pl.when(s < count[meta[first + k]])(act)

        for k in range(n):
            for s in range(SLOTS):

                def begin(k=k, s=s):
                    w_copy(k, s).start()
                    for p in range(starts[k], starts[k + 1]):
                        v_copy(p, s).start()

                each(k, s, begin)

        core, xl = meta[CORE], meta[XLO]
        half = 0
        for k in range(n):
            for p in range(starts[k], starts[k + 1]):
                width = pieces[p][2]
                for s in range(SLOTS):

                    def add(k=k, s=s, p=p, width=width):
                        if p == starts[k]:
                            w_copy(k, s).wait()
                        v_copy(p, s).wait()
                        part = jnp.dot(
                            w_buf[k * SLOTS + s], v_buf[p * SLOTS + s, :, :width], preferred_element_type=F32
                        ).reshape(rows // 64, 2, 2, 16, width)
                        if s == 0:
                            acc_ref[..., :width] = part
                        else:
                            acc_ref[..., :width] += part

                    each(k, s, add)
                for column in range(0, width, HALF):
                    for r, at in ((0, 0), (1, 1)) if both else ((0, xl), (1, 1 - xl)):
                        keep_ref[:, r, half] = acc_ref[:, at, core, :, column : column + HALF]
                        send_ref[:, r, half] = acc_ref[:, at, 1 - core, :, column : column + HALF]
                    half += 1

    out = jax.ShapeDtypeStruct((rows // 64, 2, halves, 16, HALF), F32)
    blank = pl.BlockSpec(memory_space=pl.ANY)
    whole = pl.BlockSpec(memory_space=pltpu.VMEM)
    return pl.pallas_call(
        body,
        out_shape=(out, out),
        grid_spec=pltpu.PrefetchScalarGridSpec(
            num_scalar_prefetch=3,
            in_specs=[blank] * (1 + len(arrays)),
            out_specs=(whole, whole),
            scratch_shapes=[
                pltpu.VMEM((n * SLOTS, rows, WIDTH), walk.dtype),
                pltpu.VMEM((len(pieces) * SLOTS, WIDTH, widest), walk.dtype),
                pltpu.VMEM((rows // 64, 2, 2, 16, widest), F32),
                pltpu.SemaphoreType.DMA((n * SLOTS,)),
                pltpu.SemaphoreType.DMA((len(pieces) * SLOTS,)),
            ],
        ),
    )(*scalars, walk, *arrays)


def squares(meta, ends, first, before=()):
    spots = [(p, half) for p, panel in enumerate(PANELS) for half in panel[2]]
    terms = [len(end) for end in ends]
    last = bool(before)

    def body(meta, *refs):
        olds, refs = refs[: len(before)], refs[len(before) :]
        sq_ref, sum_ref = refs[sum(terms) : sum(terms) + 2]
        row_ref = refs[-1] if last else sum_ref
        if last:
            sq_ref[...] = olds[0][...]
            row_ref[...] = olds[1][...]
        e, ref = first, 0
        for m in terms:
            for j in range(refs[ref].shape[0]):
                x = refs[ref][j]
                for k in range(1, m):
                    x = x + refs[ref + k][j]
                x = x * x
                p, half = spots[e]
                at = pl.multiple_of(meta[p] * WIDTH + half * HALF, HALF)
                sq_ref[:, pl.ds(at, HALF)] = x
                total = jnp.sum(x, axis=0, keepdims=True)
                row_ref[pl.ds(at // 128, 1)] = total[:, :128]
                row_ref[pl.ds(at // 128 + 1, 1)] = total[:, 128:]
                e += 1
            ref += m
        if last:
            sum_ref[...] = jnp.broadcast_to(row_ref[...][None], sum_ref.shape)

    whole = pl.BlockSpec(memory_space=pltpu.VMEM)
    sums = jax.ShapeDtypeStruct((16, 32, 128) if last else (32, 128), F32)
    return pl.pallas_call(
        body,
        out_shape=(jax.ShapeDtypeStruct((16, 4096), F32), sums),
        grid_spec=pltpu.PrefetchScalarGridSpec(
            num_scalar_prefetch=1,
            in_specs=[whole] * (len(before) + sum(terms)),
            out_specs=(whole, whole),
            scratch_shapes=[pltpu.VMEM((32, 128), F32)] if last else [],
        ),
    )(meta, *before, *itertools.chain(*ends))


def scaled(squared, sums):
    def body(sq_ref, sum_ref, out_ref):
        total = sum_ref[0]
        for t in range(1, sums.shape[0]):
            total = total + sum_ref[t]
        scale = total / 4096 + 1e-06
        for r in range(32):
            at = slice(r * 128, r * 128 + 128)
            out_ref[:, at] = sq_ref[:, at] / scale[r : r + 1]

    return pl.pallas_call(body, out_shape=jax.ShapeDtypeStruct(squared.shape, F32), name="scaled")(squared, sums)


def encode(totals):
    peers = totals[0].shape[0]
    codes, scales = [], []
    for total in totals:
        top = jnp.max(jnp.abs(total), axis=(*range(total.ndim - 3), total.ndim - 2))
        scale = lax.reduce_precision(jnp.maximum(top * (SCALE * 1.002), 6.2e-05), 5, 10)
        t = total * (SCALE / scale)[:, None]
        codes.append((t * jnp.abs(t) * TOP).astype(WIRE).reshape(peers, -1, HALF))
        scales.append(scale.astype(WIRE))
    rows = jnp.concatenate(scales)
    rows = jnp.pad(rows, ((0, 8 - rows.shape[0]), (0, 0)))
    return jnp.concatenate([*codes, jnp.broadcast_to(rows[None], (peers, 8, HALF))], axis=1)


def decode(coded, shapes):
    peers, end = coded.shape[0], coded.shape[1] - 8
    row, spot, sums = 0, end, []
    for shape in shapes:
        rows, n = math.prod(shape[:-1]), shape[-3]
        codes = coded[:, row : row + rows].astype(F32).reshape(peers, *shape)
        scale = coded[:, spot : spot + n].astype(F32) * (1 / SCALE)
        scale = scale.reshape(peers, *([1] * (len(shape) - 3)), n, 1, HALF)
        size = jnp.sqrt(jnp.abs(codes) * (1 / TOP))
        sums.append(jnp.sum(jnp.where(codes < 0, -size, size) * scale, axis=0))
        row, spot = row + rows, spot + n
    return sums


def pipeline(walk, values, col_index, col_count):
    meta = coordinates()
    scalars = (meta, col_index.reshape(-1), col_count.reshape(-1))

    def move(x, **by):
        return send(x, **by)

    def whole(array):
        return [(array, 0, WIDTH)]

    def pair(left, right):
        return [(left, 0, HALF), (right, 0, HALF)]

    def one(array):
        return [(array, 0, HALF)]

    ends = []

    def partial(batch, given, both=False):
        keep, give = product(batch, scalars, walk, given, both)
        return keep + move(give, dc=1)

    def exchange(totals, both=False):
        if both:
            totals = [t.reshape(16, *t.shape[2:]) for t in totals]
        arrived = lax.all_to_all(encode(totals), ("z", "xl") if both else "z", 0, 0, tiled=True)
        sums = decode(arrived, [t.shape[1:] for t in totals])
        for total in sums:
            ends.append((total,) if both else (total[0], move(total[1], dxl=1)))

    own = (values[:, :HALF], values[:, HALF:])
    up = [move(own[t], dy=1) for t in range(2)]
    down = [move(own[t], dy=3) for t in range(2)]
    over = [move(own[t], dxh=1) for t in range(2)]
    far = [move(up[0], dy=1), move(down[1], dy=3)]
    over_up = [move(over[t], dy=1) for t in range(2)]
    over_down = [move(over[t], dy=3) for t in range(2)]
    over_far = [move(far[t], dxh=1) for t in range(2)]

    exchange([partial(0, [whole(values)])])
    exchange([partial(1, [pair(*up), pair(*down), pair(*over)])])
    exchange([partial(2, [one(over_up[0]), one(over_down[0]), one(over_far[0])])])
    last = [partial(3, [pair(*far)], both=True)]
    last.append(partial(4, [one(over_up[1]), one(over_down[1]), one(over_far[1])], both=True))
    exchange(last, both=True)

    before = squares(meta, ends[:3], 0)
    squared, sums = squares(meta, ends[3:], sum(end[0].shape[0] for end in ends[:3]), before)
    sums = jnp.sum(lax.all_to_all(sums, ("z", "xl"), 0, 0), axis=0)
    sums = lax.all_to_all(jnp.broadcast_to(sums[None], (16, 32, 128)), ("xh", "y", "core"), 0, 0)
    return scaled(squared, sums)


def solution(mesh):
    fine = Mesh(mesh.devices.reshape(SIZES), AXES)
    blk, group = ("xh", "y"), ("z", "xl", "core")
    return jax.shard_map(
        pipeline,
        mesh=fine,
        in_specs=(P(blk, group), P(group, blk), P(group, None), P(group, None)),
        out_specs=P((*blk, *group), None),
        check_vma=False,
    )
```

```python
import itertools
import math

import jax
import jax.numpy as jnp
import numpy as np
from jax import lax
from jax.experimental import pallas as pl
from jax.experimental.pallas import tpu as pltpu
from jax.sharding import Mesh
from jax.sharding import PartitionSpec as P


AXES = ("xh", "y", "z", "xl", "core")
SIZES = (2, 4, 8, 2, 2)
SLOTS = 3
WIDTH = 512
HALF = 256
F32 = jnp.float32
WIRE = jnp.float16
TOP = 60000.0
SCALE = 64.0

BATCHES = (
    ((0, 0, (0, 1)),),
    ((0, 3, (0, 1)), (0, 1, (0, 1)), (1, 0, (0, 1))),
    ((1, 3, (0,)), (1, 1, (0,)), (1, 2, (0,))),
    ((0, 2, (0, 1)),),
    ((1, 3, (1,)), (1, 1, (1,)), (1, 2, (1,))),
)
PANELS = tuple(itertools.chain(*BATCHES))
CORE, XLO = len(PANELS), len(PANELS) + 1


def moves(dxh=0, dy=0, dz=0, dxl=0, dc=0):
    pairs = []
    for at in itertools.product(*(range(n) for n in SIZES)):
        to = [(a + d) % n for a, d, n in zip(at, (dxh, dy, dz, dxl, dc), SIZES)]
        pairs.append((int(np.ravel_multi_index(at, SIZES)), int(np.ravel_multi_index(to, SIZES))))
    return pairs


def send(x, **by):
    return lax.ppermute(x, AXES, moves(**by))


def coordinates():
    dx = np.array([p[0] for p in PANELS] + [0, 0], np.int32)
    dy = np.array([p[1] for p in PANELS] + [0, 0], np.int32)
    spot = np.arange(len(dx), dtype=np.int32)
    xh, y, xl, core = (lax.axis_index(name).astype(jnp.int32) for name in ("xh", "y", "xl", "core"))
    panels = ((xh ^ dx) * 4 + ((y + dy) & 3)) * (spot < CORE).astype(np.int32)
    return panels + core * (spot == CORE) + xl * (spot == XLO)


def product(batch, scalars, walk, values, both):
    panels = BATCHES[batch]
    first = sum(len(b) for b in BATCHES[:batch])
    rows = walk.shape[0]
    arrays = []
    pieces = []
    for given in values:
        for array, column, width in given:
            known = [i for i, a in enumerate(arrays) if a is array]
            if not known:
                arrays.append(array)
            pieces.append((known[0] if known else len(arrays) - 1, column, width))
    per_panel = [len(given) for given in values]
    starts = np.cumsum([0] + per_panel)
    halves = sum(p[2] for p in pieces) // HALF
    widest = max(p[2] for p in pieces)
    n = len(panels)

    def body(meta, index, count, w_hbm, *refs):
        v_hbm = refs[: len(arrays)]
        keep_ref, send_ref, w_buf, v_buf, acc_ref, w_sem, v_sem = refs[len(arrays) :]

        def w_copy(k, s):
            block = index[s * 8 + meta[first + k]]
            source = w_hbm.at[:, pl.ds(pl.multiple_of(block * WIDTH, WIDTH), WIDTH)]
            return pltpu.make_async_copy(source, w_buf.at[k * SLOTS + s], w_sem.at[k * SLOTS + s])

        def v_copy(p, s):
            array, column, width = pieces[p]
            source = v_hbm[array].at[pl.ds(s * WIDTH, WIDTH), pl.ds(column, width)]
            return pltpu.make_async_copy(source, v_buf.at[p * SLOTS + s, :, pl.ds(0, width)], v_sem.at[p * SLOTS + s])

        def each(k, s, act):
            if s == 0:
                act()
            else:
                pl.when(s < count[meta[first + k]])(act)

        for k in range(n):
            for s in range(SLOTS):

                def begin(k=k, s=s):
                    w_copy(k, s).start()
                    for p in range(starts[k], starts[k + 1]):
                        v_copy(p, s).start()

                each(k, s, begin)

        core, xl = meta[CORE], meta[XLO]
        half = 0
        for k in range(n):
            for p in range(starts[k], starts[k + 1]):
                width = pieces[p][2]
                for s in range(SLOTS):

                    def add(k=k, s=s, p=p, width=width):
                        if p == starts[k]:
                            w_copy(k, s).wait()
                        v_copy(p, s).wait()
                        part = jnp.dot(
                            w_buf[k * SLOTS + s], v_buf[p * SLOTS + s, :, :width], preferred_element_type=F32
                        ).reshape(rows // 64, 2, 2, 16, width)
                        if s == 0:
                            acc_ref[..., :width] = part
                        else:
                            acc_ref[..., :width] += part

                    each(k, s, add)
                for column in range(0, width, HALF):
                    for r, at in ((0, 0), (1, 1)) if both else ((0, xl), (1, 1 - xl)):
                        keep_ref[:, r, half] = acc_ref[:, at, core, :, column : column + HALF]
                        send_ref[:, r, half] = acc_ref[:, at, 1 - core, :, column : column + HALF]
                    half += 1

    out = jax.ShapeDtypeStruct((rows // 64, 2, halves, 16, HALF), F32)
    blank = pl.BlockSpec(memory_space=pl.ANY)
    whole = pl.BlockSpec(memory_space=pltpu.VMEM)
    return pl.pallas_call(
        body,
        out_shape=(out, out),
        grid_spec=pltpu.PrefetchScalarGridSpec(
            num_scalar_prefetch=3,
            in_specs=[blank] * (1 + len(arrays)),
            out_specs=(whole, whole),
            scratch_shapes=[
                pltpu.VMEM((n * SLOTS, rows, WIDTH), walk.dtype),
                pltpu.VMEM((len(pieces) * SLOTS, WIDTH, widest), walk.dtype),
                pltpu.VMEM((rows // 64, 2, 2, 16, widest), F32),
                pltpu.SemaphoreType.DMA((n * SLOTS,)),
                pltpu.SemaphoreType.DMA((len(pieces) * SLOTS,)),
            ],
        ),
    )(*scalars, walk, *arrays)


def squares(meta, ends, first, before=()):
    spots = [(p, half) for p, panel in enumerate(PANELS) for half in panel[2]]
    terms = [len(end) for end in ends]
    last = bool(before)

    def body(meta, *refs):
        olds, refs = refs[: len(before)], refs[len(before) :]
        sq_ref, sum_ref = refs[sum(terms) : sum(terms) + 2]
        row_ref = refs[-1] if last else sum_ref
        if last:
            sq_ref[...] = olds[0][...]
            row_ref[...] = olds[1][...]
        e, ref = first, 0
        for m in terms:
            for j in range(refs[ref].shape[0]):
                x = refs[ref][j]
                for k in range(1, m):
                    x = x + refs[ref + k][j]
                x = x * x
                p, half = spots[e]
                at = pl.multiple_of(meta[p] * WIDTH + half * HALF, HALF)
                sq_ref[:, pl.ds(at, HALF)] = x
                total = jnp.sum(x, axis=0, keepdims=True)
                row_ref[pl.ds(at // 128, 1)] = total[:, :128]
                row_ref[pl.ds(at // 128 + 1, 1)] = total[:, 128:]
                e += 1
            ref += m
        if last:
            sum_ref[...] = jnp.broadcast_to(row_ref[...][None], sum_ref.shape)

    whole = pl.BlockSpec(memory_space=pltpu.VMEM)
    sums = jax.ShapeDtypeStruct((16, 32, 128) if last else (32, 128), F32)
    return pl.pallas_call(
        body,
        out_shape=(jax.ShapeDtypeStruct((16, 4096), F32), sums),
        grid_spec=pltpu.PrefetchScalarGridSpec(
            num_scalar_prefetch=1,
            in_specs=[whole] * (len(before) + sum(terms)),
            out_specs=(whole, whole),
            scratch_shapes=[pltpu.VMEM((32, 128), F32)] if last else [],
        ),
    )(meta, *before, *itertools.chain(*ends))


def scaled(squared, sums):
    def body(sq_ref, sum_ref, out_ref):
        total = sum_ref[0]
        for t in range(1, sums.shape[0]):
            total = total + sum_ref[t]
        scale = total / 4096 + 1e-06
        for r in range(32):
            at = slice(r * 128, r * 128 + 128)
            out_ref[:, at] = sq_ref[:, at] / scale[r : r + 1]

    return pl.pallas_call(body, out_shape=jax.ShapeDtypeStruct(squared.shape, F32), name="scaled")(squared, sums)


def encode(totals):
    peers = totals[0].shape[0]
    codes, scales = [], []
    for total in totals:
        top = jnp.max(jnp.abs(total), axis=(*range(total.ndim - 3), total.ndim - 2))
        scale = lax.reduce_precision(jnp.maximum(top * (SCALE * 1.002), 6.2e-05), 5, 10)
        t = total * (SCALE / scale)[:, None]
        codes.append((t * jnp.abs(t) * TOP).astype(WIRE).reshape(peers, -1, HALF))
        scales.append(scale.astype(WIRE))
    rows = jnp.concatenate(scales)
    rows = jnp.pad(rows, ((0, 8 - rows.shape[0]), (0, 0)))
    return jnp.concatenate([*codes, jnp.broadcast_to(rows[None], (peers, 8, HALF))], axis=1)


def decode(coded, shapes):
    peers, end = coded.shape[0], coded.shape[1] - 8
    row, spot, sums = 0, end, []
    for shape in shapes:
        rows, n = math.prod(shape[:-1]), shape[-3]
        codes = coded[:, row : row + rows].astype(F32).reshape(peers, *shape)
        scale = coded[:, spot : spot + n].astype(F32) * (1 / SCALE)
        scale = scale.reshape(peers, *([1] * (len(shape) - 3)), n, 1, HALF)
        size = jnp.sqrt(jnp.abs(codes) * (1 / TOP))
        sums.append(jnp.sum(jnp.where(codes < 0, -size, size) * scale, axis=0))
        row, spot = row + rows, spot + n
    return sums


def pipeline(walk, values, col_index, col_count):
    meta = coordinates()
    scalars = (meta, col_index.reshape(-1), col_count.reshape(-1))

    def move(x, **by):
        return send(x, **by)

    def whole(array):
        return [(array, 0, WIDTH)]

    def pair(left, right):
        return [(left, 0, HALF), (right, 0, HALF)]

    def one(array):
        return [(array, 0, HALF)]

    ends = []

    def partial(batch, given, both=False):
        keep, give = product(batch, scalars, walk, given, both)
        return keep + move(give, dc=1)

    def exchange(totals, both=False):
        if both:
            totals = [t.reshape(16, *t.shape[2:]) for t in totals]
        arrived = lax.all_to_all(encode(totals), ("z", "xl") if both else "z", 0, 0, tiled=True)
        sums = decode(arrived, [t.shape[1:] for t in totals])
        for total in sums:
            ends.append((total,) if both else (total[0], move(total[1], dxl=1)))

    own = (values[:, :HALF], lax.optimization_barrier(values)[:, HALF:])
    up = [move(own[t], dy=1) for t in range(2)]
    down = [move(own[t], dy=3) for t in range(2)]
    over = [move(own[t], dxh=1) for t in range(2)]
    far = [move(up[0], dy=1), move(down[1], dy=3)]
    over_up = [move(over[t], dy=1) for t in range(2)]
    over_down = [move(over[t], dy=3) for t in range(2)]
    over_far = [move(far[t], dxh=1) for t in range(2)]

    exchange([partial(0, [whole(values)])])
    exchange([partial(1, [pair(*up), pair(*down), pair(*over)])])
    third = partial(3, [pair(*far)])
    exchange([partial(2, [one(over_up[0]), one(over_down[0]), one(over_far[0])]), third])
    exchange([partial(4, [one(over_up[1]), one(over_down[1]), one(over_far[1])], both=True)], both=True)

    before = squares(meta, ends[:4], 0)
    squared, sums = squares(meta, ends[4:], sum(end[0].shape[0] for end in ends[:4]), before)
    sums = jnp.sum(lax.all_to_all(sums, ("z", "xl"), 0, 0), axis=0)
    sums = lax.all_to_all(jnp.broadcast_to(sums[None], (16, 32, 128)), ("xh", "y", "core"), 0, 0)
    return scaled(squared, sums)


def solution(mesh):
    fine = Mesh(mesh.devices.reshape(SIZES), AXES)
    blk, group = ("xh", "y"), ("z", "xl", "core")
    return jax.shard_map(
        pipeline,
        mesh=fine,
        in_specs=(P(blk, group), P(group, blk), P(group, None), P(group, None)),
        out_specs=P((*blk, *group), None),
        check_vma=False,
    )
```
